256 devices in a mesh: gz: 32 (over x, z_hi, core), ord: 8 (over y, z_lo).
Axes of the slice: x: 4, y: 4, z: 8 (z_hi: 4, z_lo: 2; z = z_hi * 2 + z_lo), core: 2. Of those that a mesh axis runs over, the one named last changes fastest.
Arguments:
- initial: float32 [96, 64, 128, 128], P('ord', 'gz'), may hold values from -1 to 1
- cotangent: float32 [96, 64, 128, 128], P('ord', 'gz'), may hold values from -6 to 6
- mobility: float32 [96], P('ord'), may hold values from 0.05 to 0.15
- stiffness: float32 [96], P('ord'), may hold values from 0.5 to 1
Outputs:
- adjoint_initial: float32 [96, 64, 128, 128], P('ord', 'gz')
The draws below stay inside these ranges and needn't reach their ends.
All inputs are finite; a program needn't handle non-finite values.
Results may differ from the reference program's by a relative error of at most 0.00002.
Values sent between devices are 32-bit elements; how exact they have to be, the bound alone decides.
A program may use at most 128 MiB of HBM per device.

```python
import math
import jax
import jax.numpy as jnp

P_SIZE = 96
NX = 128
NY = 128
NZ = 64


def block_levels(stream_key, shape, pieces, low, largest):
    def one(position, parts):
        draws = jax.random.uniform(jax.random.fold_in(jax.random.fold_in(stream_key, 6), position), (parts,), jnp.float32, low / len(pieces), largest / len(pieces))
        return jnp.repeat(jnp.exp(draws), shape[position] // parts).reshape((-1,) + (1,) * (len(shape) - position - 1))

    factor_of = one(*pieces[0])
    for cut in pieces[1:]:
        factor_of = factor_of * one(*cut)
    return factor_of


def centred(own_key, shape, deviation, limit, split=(), kind=jnp.bfloat16):
    result = deviation * jax.random.normal(own_key, shape, jnp.float32)
    if split:
        result = result * block_levels(own_key, shape, split, -0.22, 0.18)
    return jnp.clip(result, -limit, limit).astype(kind)


def setup_inputs(seed: int = 0) -> dict:
    splits = jax.random.split(jax.random.key(seed), 5)
    initial = jnp.clip(jax.random.uniform(splits[0], (P_SIZE, NZ, NX, NY), jnp.float32, -1.0, 1.0) * block_levels(splits[0], (P_SIZE, NZ, NX, NY), ((0, 8), (1, 32)), -0.4, 0.0), -1.0, 1.0)
    cotangent = centred(splits[1], (P_SIZE, NZ, NX, NY), 1.0, 6.0, ((0, 8), (1, 32)), jnp.float32)
    mobility = jnp.clip(jnp.exp(math.log(0.15) - 1.0986123 * jax.random.uniform(splits[2], (P_SIZE,), jnp.float32) ** block_levels(splits[2], (P_SIZE,), ((0, 8),), -0.2, 0.2)), 0.05, 0.15)
    stiffness = jnp.clip(jnp.exp(math.log(1.0) - 0.6931472 * jax.random.uniform(splits[3], (P_SIZE,), jnp.float32) ** block_levels(splits[3], (P_SIZE,), ((0, 8),), -0.2, 0.2)), 0.5, 1.0)
    return dict(initial=initial, cotangent=cotangent, mobility=mobility, stiffness=stiffness)


couple_scale = 2.0


def laplacian(values):
    summed = -6.0 * values
    for axis_num in (1, 2, 3):
        summed = summed + jnp.roll(values, 1, axis_num) + jnp.roll(values, -1, axis_num)
    return summed


def forward(values, squares, rate_col, stiff_col, coupling):
    potential = -values + values * values * values + 2.0 * coupling * values * (squares - values * values) - stiff_col * laplacian(values)
    return values - rate_col * potential


def backward(values, adjoint, squares, rate_col, stiff_col, coupling):
    scaled = rate_col * adjoint
    coupled = jnp.sum(values * scaled, 0)
    well_slope = -1.0 + 3.0 * values * values + 2.0 * coupling * squares - 6.0 * coupling * values * values
    return adjoint - (well_slope * scaled + 4.0 * coupling * values * coupled - stiff_col * laplacian(scaled))


def reference(initial, cotangent, mobility, stiffness):
    coupling = couple_scale / P_SIZE
    rate_col = mobility.reshape(-1, 1, 1, 1)
    stiff_col = stiffness.reshape(-1, 1, 1, 1)
    squares_first = jnp.sum(initial * initial, 0)
    middle = forward(initial, squares_first, rate_col, stiff_col, coupling)
    squares_second = jnp.sum(middle * middle, 0)
    adjoint_middle = backward(middle, cotangent, squares_second, rate_col, stiff_col, coupling)
    return backward(initial, adjoint_middle, squares_first, rate_col, stiff_col, coupling)
```

```python
import functools

import jax
import jax.numpy as jnp
from jax import lax
from jax.experimental import pallas as pl
from jax.experimental.pallas import tpu as pltpu
from jax.sharding import PartitionSpec as P

P_SIZE = 96
COUPLE = 2.0 / P_SIZE
CUBE = 3.0 - 6.0 * COUPLE
MESH = pl.DeviceIdType.MESH
HALVES = 2


def flat_laplacian(plane, other):
    rows, cols = plane.shape
    side = pltpu.roll(plane, 1, 0) + pltpu.roll(plane, rows - 1, 0)
    side = side + (pltpu.roll(plane, 1, 1) + pltpu.roll(plane, cols - 1, 1))
    return side + (other - 6.0 * plane)


def kernel(
    n_gz, n_y,
    u_hbm, a_hbm, rate_hbm, stiff_hbm,
    part, w_halo,
    rate, stiff, u, a, mid, adj, w, u_halo, a_halo, partial, parts, half_sum, half_in, total, result,
    load_sem, far_send, far_recv, near_send, near_recv,
    in_send, in_recv, mid_send, mid_recv, out_send, out_recv, store_sem,
):
    order, planes, nx, ny = u.shape
    gz, ord_ = lax.axis_index("gz"), lax.axis_index("ord")
    core, y, zl = lax.rem(gz, 2), ord_ // 2, lax.rem(ord_, 2)
    sibling = gz + 1 - 2 * core
    chip = gz - core
    far = lax.rem(jnp.where(core == 1, gz + 1, gz + n_gz - 1), n_gz)
    far_plane, near_plane = core, 1 - core
    reducer = core == zl
    half_rows = nx // HALVES

    def at(gz_=None, y_=None, zl_=None):
        y_ = y if y_ is None else y_
        zl_ = zl if zl_ is None else zl_
        return {"gz": gz if gz_ is None else gz_, "ord": 2 * y_ + zl_}

    loads = [
        pltpu.make_async_copy(u_hbm, u, load_sem.at[0]),
        pltpu.make_async_copy(a_hbm, a, load_sem.at[1]),
        pltpu.make_async_copy(rate_hbm, rate, load_sem.at[2]),
        pltpu.make_async_copy(stiff_hbm, stiff, load_sem.at[3]),
    ]
    for copy in loads:
        copy.start()

    barrier = pltpu.get_barrier_semaphore()
    peers = [at(far), at(sibling, zl_=1 - zl), at(sibling)]
    for step in range(1, n_y):
        for c in range(2):
            peers.append(at(chip + c, lax.rem(y + step, n_y)))
    for peer in peers:
        pl.semaphore_signal(barrier, inc=1, device_id=peer, device_id_type=MESH)
    pl.semaphore_wait(barrier, len(peers))

    def halo(index, src, dst, far_side, rows):
        mine = far_plane if far_side else near_plane
        theirs = 1 - mine
        return pltpu.make_async_remote_copy(
            src_ref=src.at[:, mine, rows],
            dst_ref=dst.at[:, theirs, rows],
            send_sem=(far_send if far_side else near_send).at[index],
            recv_sem=(far_recv if far_side else near_recv).at[index],
            device_id=at(far if far_side else sibling),
            device_id_type=MESH,
        )

    def half(h):
        return pl.ds(h * half_rows, half_rows)

    u_far = [halo(h, u_hbm, u_halo, True, half(h)) for h in range(HALVES)]
    a_far = [halo(HALVES + h, a_hbm, a_halo, True, half(h)) for h in range(HALVES)]
    w_far = [halo(2 * HALVES + h, w, w_halo, True, half(h)) for h in range(HALVES)]
    u_near = halo(0, u_hbm, u_halo, False, pl.ds(0, nx))
    a_near = halo(1, a_hbm, a_halo, False, pl.ds(0, nx))
    w_near = [halo(2 + h, w, w_halo, False, half(h)) for h in range(HALVES)]
    for copy in u_far + [u_near] + a_far:
        copy.start()

    class Total:
        def __init__(self, call, sums, first, rows):
            self.call, self.sums, self.first, self.quarter = call, sums, first, rows // n_y

        def rows(self, y_):
            return pl.ds(pl.multiple_of(self.first + y_ * self.quarter, 8), self.quarter)

        def block(self, ref, *lead):
            return ref.at[(*lead, pl.ds(0, self.sums), slice(None), pl.ds(0, self.quarter))]

        def source(self, y_):
            return partial.at[pl.ds(0, self.sums), :, self.rows(y_)]

        def gather(self, step, from_core):
            to = lax.rem(y + step, n_y)
            return pltpu.make_async_remote_copy(
                src_ref=self.source(to),
                dst_ref=self.block(parts, self.call, from_core, step),
                send_sem=in_send.at[self.call, step],
                recv_sem=in_recv.at[self.call, from_core, step],
                device_id=at(chip + zl, to),
                device_id_type=MESH,
            )

        def swap(self):
            return pltpu.make_async_remote_copy(
                src_ref=self.block(half_sum, self.call, slice(None)),
                dst_ref=self.block(half_in, self.call, slice(None)),
                send_sem=mid_send.at[self.call],
                recv_sem=mid_recv.at[self.call],
                device_id=at(sibling, zl_=1 - zl),
                device_id_type=MESH,
            )

        def spread(self, step, to_core, from_step=None):
            return pltpu.make_async_remote_copy(
                src_ref=self.block(total, self.call, to_core),
                dst_ref=result.at[self.call, pl.ds(0, self.sums), :, self.rows(y)],
                send_sem=out_send.at[self.call, to_core, step],
                recv_sem=out_recv.at[self.call, step],
                device_id=at(chip + to_core, lax.rem(y + step, n_y)),
                device_id_type=MESH,
            )

        def arriving(self, step):
            from_ = lax.rem(y + n_y - step, n_y)
            return pltpu.make_async_remote_copy(
                src_ref=self.block(total, self.call, core),
                dst_ref=result.at[self.call, pl.ds(0, self.sums), :, self.rows(from_)],
                send_sem=out_send.at[self.call, core, step],
                recv_sem=out_recv.at[self.call, step],
                device_id=at(),
                device_id_type=MESH,
            )

        def send(self):
            for step in range(1, n_y):
                self.gather(step, core).start()

            @pl.when(jnp.logical_not(reducer))
            def _():
                self.gather(0, core).start()

        def reduce(self):
            @pl.when(reducer)
            def _():
                self.block(parts, self.call, core, 0)[...] = self.source(y)[...]
                self.gather(0, 1 - core).wait_recv()
                for step in range(1, n_y):
                    for c in range(2):
                        self.gather(step, c).wait_recv()
                for c in range(2):
                    block = self.block(parts, self.call, c, 0)[...]
                    for step in range(1, n_y):
                        block = block + self.block(parts, self.call, c, step)[...]
                    self.block(half_sum, self.call, c)[...] = block
                self.swap().start()

        def finish(self):
            @pl.when(reducer)
            def _():
                self.swap().wait_recv()
                for c in range(2):
                    self.block(total, self.call, c)[...] = (
                        self.block(half_sum, self.call, c)[...] + self.block(half_in, self.call, c)[...]
                    )
                for step in range(1, n_y):
                    for c in range(2):
                        self.spread(step, c).start()
                self.spread(0, 1 - core).start()
                result[self.call, pl.ds(0, self.sums), :, self.rows(y)] = self.block(total, self.call, core)[...]

        def arrive(self):
            for step in range(1, n_y):
                self.arriving(step).wait_recv()

            @pl.when(jnp.logical_not(reducer))
            def _():
                self.arriving(0).wait_recv()

        def drain(self):
            for step in range(1, n_y):
                self.gather(step, core).wait_send()

            @pl.when(jnp.logical_not(reducer))
            def _():
                self.gather(0, core).wait_send()

            @pl.when(reducer)
            def _():
                self.swap().wait_send()
                for step in range(1, n_y):
                    for c in range(2):
                        self.spread(step, c).wait_send()
                self.spread(0, 1 - core).wait_send()

    squares_first = Total(0, 1, 0, nx)
    second = [Total(1 + h, 2, h * half_rows, half_rows) for h in range(HALVES)]
    coupled_first = [Total(1 + HALVES + h, 1, h * half_rows, half_rows) for h in range(HALVES)]

    loads[0].wait()
    for z in range(planes):

        def add_square(p, acc):
            value = u[p, z]
            return acc + value * value

        partial[0, z] = lax.fori_loop(0, order, add_square, jnp.zeros((nx, ny), jnp.float32))
    squares_first.send()
    a_near.start()

    loads[2].wait()
    loads[3].wait()

    def own_middle(i, _):
        p, z = i // planes, lax.rem(i, planes)
        value = u[p, z]
        m, k = rate[p], stiff[p]
        slope = (1.0 + m) - (m * (1.0 - 2.0 * COUPLE)) * (value * value)
        mid[p, z] = value * slope + (m * k) * flat_laplacian(value, u[p, 1 - z])
        return 0

    lax.fori_loop(0, order * planes, own_middle, 0)
    squares_first.reduce()

    loads[1].wait()

    def own_adjoint(i, _):
        p, z = i // planes, lax.rem(i, planes)
        value = a[p, z]
        m, k = rate[p], stiff[p]
        adj[p, z] = (1.0 + m) * value + (m * k) * flat_laplacian(value, a[p, 1 - z])
        return 0

    lax.fori_loop(0, order * planes, own_adjoint, 0)
    squares_first.finish()
    squares_first.arrive()
    squares_first.drain()

    u_near.wait_recv()
    for h in range(HALVES):
        rows = half(h)
        u_far[h].wait_recv()
        for z in range(planes):
            weight = (2.0 * COUPLE) * result[0, 0, z, rows]

            def middle(p, carry):
                squares, coupled = carry
                m, k = rate[p], stiff[p]
                value = mid[p, z, rows] - m * (u[p, z, rows] * weight)
                value = value + (m * k) * u_halo[p, z, rows]
                mid[p, z, rows] = value
                return squares + value * value, coupled + value * (m * a[p, z, rows])

            zero = jnp.zeros((half_rows, ny), jnp.float32)
            squares, coupled = lax.fori_loop(0, order, middle, (zero, zero))
            partial[0, z, rows] = squares
            partial[1, z, rows] = coupled
        second[h].send()
        second[h].reduce()
        second[h].finish()
        second[h].arrive()
        second[h].drain()

    a_near.wait_recv()
    for h in range(HALVES):
        rows = half(h)
        a_far[h].wait_recv()
        for z in range(planes):
            weight = (2.0 * COUPLE) * result[1 + h, 0, z, rows]
            pull = (4.0 * COUPLE) * result[1 + h, 1, z, rows]

            def adjoint(p, acc):
                m, k = rate[p], stiff[p]
                field = mid[p, z, rows]
                value = adj[p, z, rows] - (m * a[p, z, rows]) * (CUBE * (field * field) + weight)
                value = value - field * pull + (m * k) * a_halo[p, z, rows]
                adj[p, z, rows] = value
                scaled = m * value
                w[p, z, rows] = scaled
                return acc + u[p, z, rows] * scaled

            partial[0, z, rows] = lax.fori_loop(
                0, order, adjoint, jnp.zeros((half_rows, ny), jnp.float32)
            )
        w_far[h].start()
        w_near[h].start()
        coupled_first[h].send()

    for h in range(HALVES):
        coupled_first[h].reduce()

    def own_result(i, _):
        p, z = i // planes, lax.rem(i, planes)
        value, scaled = u[p, z], w[p, z]
        slope = CUBE * (value * value) + (2.0 * COUPLE) * result[0, 0, z]
        local = adj[p, z] + scaled - scaled * slope
        adj[p, z] = local + stiff[p] * flat_laplacian(scaled, w[p, 1 - z])
        return 0

    lax.fori_loop(0, order * planes, own_result, 0)
    for h in range(HALVES):
        coupled_first[h].finish()
    for h in range(HALVES):
        rows = half(h)
        coupled_first[h].arrive()
        for z in range(planes):
            pull = (4.0 * COUPLE) * result[1 + HALVES + h, 0, z, rows]

            def couple(p, _):
                adj[p, z, rows] = adj[p, z, rows] - u[p, z, rows] * pull
                return 0

            lax.fori_loop(0, order, couple, 0)
    store = pltpu.make_async_copy(adj, part, store_sem)
    store.start()
    for h in range(HALVES):
        coupled_first[h].drain()
    for copy in u_far + a_far + [u_near, a_near]:
        copy.wait_send()
    for copy in w_near + w_far:
        copy.wait()
    store.wait()


def on_device(n_gz, n_ord, initial, cotangent, mobility, stiffness):
    shape = initial.shape
    order, planes, nx, ny = shape
    n_y = n_ord // 2
    calls = 1 + 2 * HALVES
    f32 = jnp.float32
    field = jax.ShapeDtypeStruct(shape, f32)
    quarter = nx // n_y
    part, w_halo = pl.pallas_call(
        functools.partial(kernel, n_gz, n_y),
        out_shape=(field, field),
        in_specs=[pl.BlockSpec(memory_space=pltpu.HBM)] * 4,
        out_specs=[pl.BlockSpec(memory_space=pl.ANY)] * 2,
        scratch_shapes=[pltpu.SMEM((order,), f32)] * 2
        + [pltpu.VMEM(shape, f32)] * 7
        + [
            pltpu.VMEM((2, planes, nx, ny), f32),
            pltpu.VMEM((calls, 2, n_y, 2, planes, quarter, ny), f32),
            pltpu.VMEM((calls, 2, 2, planes, quarter, ny), f32),
            pltpu.VMEM((calls, 2, 2, planes, quarter, ny), f32),
            pltpu.VMEM((calls, 2, 2, planes, quarter, ny), f32),
            pltpu.VMEM((calls, 2, planes, nx, ny), f32),
            pltpu.SemaphoreType.DMA((4,)),
            pltpu.SemaphoreType.DMA((3 * HALVES,)),
            pltpu.SemaphoreType.DMA((3 * HALVES,)),
            pltpu.SemaphoreType.DMA((2 + HALVES,)),
            pltpu.SemaphoreType.DMA((2 + HALVES,)),
            pltpu.SemaphoreType.DMA((calls, n_y)),
            pltpu.SemaphoreType.DMA((calls, 2, n_y)),
            pltpu.SemaphoreType.DMA((calls,)),
            pltpu.SemaphoreType.DMA((calls,)),
            pltpu.SemaphoreType.DMA((calls, 2, n_y)),
            pltpu.SemaphoreType.DMA((calls, n_y)),
            pltpu.SemaphoreType.DMA,
        ],
        compiler_params=pltpu.CompilerParams(
            collective_id=0, has_side_effects=True, vmem_limit_bytes=32 << 20
        ),
        name="adjoint_steps",
    )(*(pltpu.with_memory_space_constraint(x, pltpu.HBM) for x in (initial, cotangent, mobility, stiffness)))
    return part + stiffness.reshape(-1, 1, 1, 1) * w_halo


def solution(mesh):
    return jax.shard_map(
        functools.partial(on_device, mesh.shape["gz"], mesh.shape["ord"]),
        mesh=mesh,
        in_specs=(P("ord", "gz", None, None), P("ord", "gz", None, None), P("ord"), P("ord")),
        out_specs=P("ord", "gz", None, None),
        check_vma=False,
    )
```

```python
import functools

import jax
import jax.numpy as jnp
from jax import lax
from jax.experimental import pallas as pl
from jax.experimental.pallas import tpu as pltpu
from jax.sharding import PartitionSpec as P

P_SIZE = 96
COUPLE = 2.0 / P_SIZE
CUBE = 3.0 - 6.0 * COUPLE
MESH = pl.DeviceIdType.MESH
HALVES = 2
SPREAD = (2, 1, 3)


def flat_laplacian(plane, other):
    rows, cols = plane.shape
    side = pltpu.roll(plane, 1, 0) + pltpu.roll(plane, rows - 1, 0)
    side = side + (pltpu.roll(plane, 1, 1) + pltpu.roll(plane, cols - 1, 1))
    return side + (other - 6.0 * plane)


def kernel(
    n_gz, n_y,
    u_hbm, a_hbm, rate_hbm, stiff_hbm,
    part, w_halo,
    rate, stiff, u, a, mid, adj, w, u_halo, a_halo, partial, parts, half_sum, half_in, total, result,
    load_sem, far_send, far_recv, near_send, near_recv,
    in_send, in_recv, mid_send, mid_recv, out_send, out_recv, store_sem,
):
    order, planes, nx, ny = u.shape
    gz, ord_ = lax.axis_index("gz"), lax.axis_index("ord")
    core, y, zl = lax.rem(gz, 2), ord_ // 2, lax.rem(ord_, 2)
    sibling = gz + 1 - 2 * core
    chip = gz - core
    far = lax.rem(jnp.where(core == 1, gz + 1, gz + n_gz - 1), n_gz)
    far_plane, near_plane = core, 1 - core
    reducer = core == zl
    half_rows = nx // HALVES

    def at(gz_=None, y_=None, zl_=None):
        y_ = y if y_ is None else y_
        zl_ = zl if zl_ is None else zl_
        return {"gz": gz if gz_ is None else gz_, "ord": 2 * y_ + zl_}

    loads = [
        pltpu.make_async_copy(u_hbm, u, load_sem.at[0]),
        pltpu.make_async_copy(a_hbm, a, load_sem.at[1]),
        pltpu.make_async_copy(rate_hbm, rate, load_sem.at[2]),
        pltpu.make_async_copy(stiff_hbm, stiff, load_sem.at[3]),
    ]
    for copy in loads:
        copy.start()

    barrier = pltpu.get_barrier_semaphore()
    peers = [at(far), at(sibling, zl_=1 - zl), at(sibling)]
    for step in range(1, n_y):
        for c in range(2):
            peers.append(at(chip + c, lax.rem(y + step, n_y)))
    for peer in peers:
        pl.semaphore_signal(barrier, inc=1, device_id=peer, device_id_type=MESH)
    pl.semaphore_wait(barrier, len(peers))

    def halo(index, src, dst, far_side, rows):
        mine = far_plane if far_side else near_plane
        theirs = 1 - mine
        return pltpu.make_async_remote_copy(
            src_ref=src.at[:, mine, rows],
            dst_ref=dst.at[:, theirs, rows],
            send_sem=(far_send if far_side else near_send).at[index],
            recv_sem=(far_recv if far_side else near_recv).at[index],
            device_id=at(far if far_side else sibling),
            device_id_type=MESH,
        )

    def half(h):
        return pl.ds(h * half_rows, half_rows)

    u_far = [halo(h, u_hbm, u_halo, True, half(h)) for h in range(HALVES)]
    a_far = [halo(HALVES + h, a_hbm, a_halo, True, half(h)) for h in range(HALVES)]
    w_far = [halo(2 * HALVES + h, w, w_halo, True, half(h)) for h in range(HALVES)]
    u_near = halo(0, u_hbm, u_halo, False, pl.ds(0, nx))
    a_near = halo(1, a_hbm, a_halo, False, pl.ds(0, nx))
    w_near = [halo(2 + h, w, w_halo, False, half(h)) for h in range(HALVES)]
    for copy in u_far + [u_near] + a_far:
        copy.start()

    class Total:
        def __init__(self, call, sums, first, rows):
            self.call, self.sums, self.first, self.quarter = call, sums, first, rows // n_y

        def rows(self, y_, count=1):
            return pl.ds(pl.multiple_of(self.first + y_ * self.quarter, 8), count * self.quarter)

        def block(self, ref, slot):
            return ref.at[self.call, slot, pl.ds(0, self.sums), :, pl.ds(0, self.quarter)]

        def source(self, y_, count=1):
            return partial.at[pl.ds(0, self.sums), :, self.rows(y_, count)]

        def target(self, y_, count=1):
            return result.at[self.call, pl.ds(0, self.sums), :, self.rows(y_, count)]

        def wait(self, ref, sem, arrival):
            copy = pltpu.make_async_remote_copy(ref, ref, sem, sem, device_id=at(sibling), device_id_type=MESH)
            (copy.wait_recv if arrival else copy.wait_send)()

        def seven(self):
            return self.block(parts, pl.ds(1, 2 * n_y - 1))

        def gather(self, step):
            to = lax.rem(y + step, n_y)
            return pltpu.make_async_remote_copy(
                src_ref=self.source(to),
                dst_ref=self.block(parts, jnp.where(reducer, 0, n_y) + step),
                send_sem=in_send.at[self.call],
                recv_sem=in_recv.at[self.call],
                device_id=at(chip + zl, to),
                device_id_type=MESH,
            )

        def swap(self):
            return pltpu.make_async_remote_copy(
                src_ref=self.block(half_sum, slice(None)),
                dst_ref=self.block(half_in, slice(None)),
                send_sem=mid_send.at[self.call],
                recv_sem=mid_recv.at[self.call],
                device_id=at(sibling, zl_=1 - zl),
                device_id_type=MESH,
            )

        def spread(self, step, group):
            return pltpu.make_async_remote_copy(
                src_ref=self.block(total, group),
                dst_ref=self.target(y),
                send_sem=out_send.at[self.call],
                recv_sem=out_recv.at[self.call],
                device_id=at(sibling if group else gz, lax.rem(y + step, n_y)),
                device_id_type=MESH,
            )

        def send(self):
            for step in SPREAD:
                self.gather(step).start()

            @pl.when(jnp.logical_not(reducer))
            def _():
                self.gather(0).start()

        def reduce(self):
            @pl.when(reducer)
            def _():
                own = self.source(y)[...]
                self.wait(self.seven(), in_recv.at[self.call], True)
                for group in range(2):
                    block = self.block(parts, n_y)[...] if group else own
                    for step in range(1, n_y):
                        block = block + self.block(parts, group * n_y + step)[...]
                    self.block(half_sum, group)[...] = block
                self.swap().start()

        def finish(self):
            @pl.when(reducer)
            def _():
                self.swap().wait_recv()
                for group in range(2):
                    block = self.block(half_sum, group)[...] + self.block(half_in, 1 - group)[...]
                    self.block(total, group)[...] = block
                    if group == 0:
                        self.target(y)[...] = block
                for step in SPREAD:
                    for group in range(2):
                        self.spread(step, group).start()
                self.spread(0, 1).start()

        def arrive(self):
            for others, count in ((reducer, n_y - 1), (jnp.logical_not(reducer), n_y)):

                @pl.when(others)
                def _():
                    self.wait(self.target(0, count), out_recv.at[self.call], True)

        def drain(self):
            for others, count in ((reducer, n_y - 1), (jnp.logical_not(reducer), n_y)):

                @pl.when(others)
                def _():
                    self.wait(self.source(0, count), in_send.at[self.call], False)

            @pl.when(reducer)
            def _():
                self.swap().wait_send()
                self.wait(self.seven(), out_send.at[self.call], False)

    squares_first = Total(0, 1, 0, nx)
    second = [Total(1 + h, 2, h * half_rows, half_rows) for h in range(HALVES)]
    coupled_first = [Total(1 + HALVES + h, 1, h * half_rows, half_rows) for h in range(HALVES)]

    loads[0].wait()
    for z in range(planes):

        def add_square(p, acc):
            value = u[p, z]
            return acc + value * value

        partial[0, z] = lax.fori_loop(0, order, add_square, jnp.zeros((nx, ny), jnp.float32))
    squares_first.send()
    a_near.start()

    loads[2].wait()
    loads[3].wait()

    def own_middle(i, _):
        p, z = i // planes, lax.rem(i, planes)
        value = u[p, z]
        m, k = rate[p], stiff[p]
        slope = (1.0 + m) - (m * (1.0 - 2.0 * COUPLE)) * (value * value)
        mid[p, z] = value * slope + (m * k) * flat_laplacian(value, u[p, 1 - z])
        return 0

    lax.fori_loop(0, order * planes, own_middle, 0)
    loads[1].wait()

    def own_adjoint(i, _):
        p, z = i // planes, lax.rem(i, planes)
        value = a[p, z]
        m, k = rate[p], stiff[p]
        adj[p, z] = (1.0 + m) * value + (m * k) * flat_laplacian(value, a[p, 1 - z])
        return 0

    lax.fori_loop(0, order, own_adjoint, 0)
    squares_first.reduce()
    lax.fori_loop(order, order * planes, own_adjoint, 0)
    squares_first.finish()
    squares_first.arrive()
    squares_first.drain()

    def middle_half(h):
        rows = half(h)
        u_far[h].wait_recv()
        for z in range(planes):
            weight = (2.0 * COUPLE) * result[0, 0, z, rows]

            def middle(p, carry):
                squares, coupled = carry
                m, k = rate[p], stiff[p]
                value = mid[p, z, rows] - m * (u[p, z, rows] * weight)
                value = value + (m * k) * u_halo[p, z, rows]
                mid[p, z, rows] = value
                return squares + value * value, coupled + value * (m * a[p, z, rows])

            zero = jnp.zeros((half_rows, ny), jnp.float32)
            squares, coupled = lax.fori_loop(0, order, middle, (zero, zero))
            partial[0, z, rows] = squares
            partial[1, z, rows] = coupled
        second[h].send()

    def adjoint_half(h):
        rows = half(h)
        a_far[h].wait_recv()
        for z in range(planes):
            weight = (2.0 * COUPLE) * result[1 + h, 0, z, rows]
            pull = (4.0 * COUPLE) * result[1 + h, 1, z, rows]

            def adjoint(p, acc):
                m, k = rate[p], stiff[p]
                field = mid[p, z, rows]
                value = adj[p, z, rows] - (m * a[p, z, rows]) * (CUBE * (field * field) + weight)
                value = value - field * pull + (m * k) * a_halo[p, z, rows]
                adj[p, z, rows] = value
                scaled = m * value
                w[p, z, rows] = scaled
                return acc + u[p, z, rows] * scaled

            partial[0, z, rows] = lax.fori_loop(
                0, order, adjoint, jnp.zeros((half_rows, ny), jnp.float32)
            )
        w_far[h].start()
        w_near[h].start()
        coupled_first[h].send()

    u_near.wait_recv()
    middle_half(0)
    second[0].reduce()
    middle_half(1)
    second[0].finish()
    second[1].reduce()
    second[0].arrive()
    second[0].drain()
    second[1].finish()
    a_near.wait_recv()
    adjoint_half(0)
    second[1].arrive()
    second[1].drain()
    coupled_first[0].reduce()
    adjoint_half(1)

    def own_result(i, _):
        p, z = i // planes, lax.rem(i, planes)
        value, scaled = u[p, z], w[p, z]
        slope = CUBE * (value * value) + (2.0 * COUPLE) * result[0, 0, z]
        local = adj[p, z] + scaled - scaled * slope
        adj[p, z] = local + stiff[p] * flat_laplacian(scaled, w[p, 1 - z])
        return 0

    coupled_first[0].finish()
    lax.fori_loop(0, order, own_result, 0)
    coupled_first[1].reduce()
    lax.fori_loop(order, order * planes, own_result, 0)
    coupled_first[1].finish()
    for h in range(HALVES):
        rows = half(h)
        coupled_first[h].arrive()
        for z in range(planes):
            pull = (4.0 * COUPLE) * result[1 + HALVES + h, 0, z, rows]

            def couple(p, _):
                adj[p, z, rows] = adj[p, z, rows] - u[p, z, rows] * pull
                return 0

            lax.fori_loop(0, order, couple, 0)
    store = pltpu.make_async_copy(adj, part, store_sem)
    store.start()
    for h in range(HALVES):
        coupled_first[h].drain()
    for copy in u_far + a_far + [u_near, a_near]:
        copy.wait_send()
    for copy in w_near + w_far:
        copy.wait()
    store.wait()


def on_device(n_gz, n_ord, initial, cotangent, mobility, stiffness):
    shape = initial.shape
    order, planes, nx, ny = shape
    n_y = n_ord // 2
    calls = 1 + 2 * HALVES
    f32 = jnp.float32
    field = jax.ShapeDtypeStruct(shape, f32)
    quarter = nx // n_y
    part, w_halo = pl.pallas_call(
        functools.partial(kernel, n_gz, n_y),
        out_shape=(field, field),
        in_specs=[pl.BlockSpec(memory_space=pltpu.HBM)] * 4,
        out_specs=[pl.BlockSpec(memory_space=pl.ANY)] * 2,
        scratch_shapes=[pltpu.SMEM((order,), f32)] * 2
        + [pltpu.VMEM(shape, f32)] * 7
        + [
            pltpu.VMEM((2, planes, nx, ny), f32),
            pltpu.VMEM((calls, 2 * n_y, 2, planes, quarter, ny), f32),
            pltpu.VMEM((calls, 2, 2, planes, quarter, ny), f32),
            pltpu.VMEM((calls, 2, 2, planes, quarter, ny), f32),
            pltpu.VMEM((calls, 2, 2, planes, quarter, ny), f32),
            pltpu.VMEM((calls, 2, planes, nx, ny), f32),
            pltpu.SemaphoreType.DMA((4,)),
            pltpu.SemaphoreType.DMA((3 * HALVES,)),
            pltpu.SemaphoreType.DMA((3 * HALVES,)),
            pltpu.SemaphoreType.DMA((2 + HALVES,)),
            pltpu.SemaphoreType.DMA((2 + HALVES,)),
        ]
        + [pltpu.SemaphoreType.DMA((calls,))] * 6
        + [
            pltpu.SemaphoreType.DMA,
        ],
        compiler_params=pltpu.CompilerParams(
            collective_id=0, has_side_effects=True, vmem_limit_bytes=32 << 20
        ),
        name="adjoint_steps",
    )(*(pltpu.with_memory_space_constraint(x, pltpu.HBM) for x in (initial, cotangent, mobility, stiffness)))
    return part + stiffness.reshape(-1, 1, 1, 1) * w_halo


def solution(mesh):
    return jax.shard_map(
        functools.partial(on_device, mesh.shape["gz"], mesh.shape["ord"]),
        mesh=mesh,
        in_specs=(P("ord", "gz", None, None), P("ord", "gz", None, None), P("ord"), P("ord")),
        out_specs=P("ord", "gz", None, None),
        check_vma=False,
    )
```

```python
import functools

import jax
import jax.numpy as jnp
from jax import lax
from jax.experimental import pallas as pl
from jax.experimental.pallas import tpu as pltpu
from jax.sharding import PartitionSpec as P

P_SIZE = 96
COUPLE = 2.0 / P_SIZE
CUBE = 3.0 - 6.0 * COUPLE
MESH = pl.DeviceIdType.MESH
HALVES = 2
SPREAD = (2, 1, 3)


def flat_laplacian(plane, other):
    rows, cols = plane.shape
    side = pltpu.roll(plane, 1, 0) + pltpu.roll(plane, rows - 1, 0)
    side = side + (pltpu.roll(plane, 1, 1) + pltpu.roll(plane, cols - 1, 1))
    return side + (other - 6.0 * plane)


def kernel(
    n_gz, n_y,
    u_hbm, a_hbm, rate_hbm, stiff_hbm,
    part, w_halo,
    rate, stiff, u, a, mid, adj, w, u_halo, a_halo, partial, parts, half_sum, half_in, total, result,
    load_sem, far_send, far_recv, near_send, near_recv,
    in_send, in_recv, mid_send, mid_recv, out_send, out_recv, store_sem, turn,
):
    order, planes, nx, ny = u.shape
    gz, ord_ = lax.axis_index("gz"), lax.axis_index("ord")
    core, y, zl = lax.rem(gz, 2), ord_ // 2, lax.rem(ord_, 2)
    sibling = gz + 1 - 2 * core
    chip = gz - core
    far = lax.rem(jnp.where(core == 1, gz + 1, gz + n_gz - 1), n_gz)
    far_plane, near_plane = core, 1 - core
    reducer = core == zl
    half_rows = nx // HALVES

    def at(gz_=None, y_=None, zl_=None):
        y_ = y if y_ is None else y_
        zl_ = zl if zl_ is None else zl_
        return {"gz": gz if gz_ is None else gz_, "ord": 2 * y_ + zl_}

    loads = [
        pltpu.make_async_copy(u_hbm, u, load_sem.at[0]),
        pltpu.make_async_copy(a_hbm, a, load_sem.at[1]),
        pltpu.make_async_copy(rate_hbm, rate, load_sem.at[2]),
        pltpu.make_async_copy(stiff_hbm, stiff, load_sem.at[3]),
    ]
    for copy in loads:
        copy.start()

    barrier = pltpu.get_barrier_semaphore()
    peers = [at(far), at(sibling, zl_=1 - zl), at(sibling), at(zl_=1 - zl)]
    for step in range(1, n_y):
        for c in range(2):
            peers.append(at(chip + c, lax.rem(y + step, n_y)))
    for peer in peers:
        pl.semaphore_signal(barrier, inc=1, device_id=peer, device_id_type=MESH)
    pl.semaphore_wait(barrier, len(peers))

    def halo(index, src, dst, far_side, rows):
        mine = far_plane if far_side else near_plane
        theirs = 1 - mine
        return pltpu.make_async_remote_copy(
            src_ref=src.at[:, mine, rows],
            dst_ref=dst.at[:, theirs, rows],
            send_sem=(far_send if far_side else near_send).at[index],
            recv_sem=(far_recv if far_side else near_recv).at[index],
            device_id=at(far if far_side else sibling),
            device_id_type=MESH,
        )

    def half(h):
        return pl.ds(h * half_rows, half_rows)

    u_far = [halo(h, u_hbm, u_halo, True, half(h)) for h in range(HALVES)]
    a_far = [halo(HALVES + h, a_hbm, a_halo, True, half(h)) for h in range(HALVES)]
    w_far = [halo(2 * HALVES + h, w, w_halo, True, half(h)) for h in range(HALVES)]
    u_near = halo(0, u_hbm, u_halo, False, pl.ds(0, nx))
    a_near = halo(1, a_hbm, a_halo, False, pl.ds(0, nx))
    w_near = [halo(2 + h, w, w_halo, False, half(h)) for h in range(HALVES)]
    for copy in u_far + [u_near]:
        copy.start()

    a_far[0].start()

    def yield_link():
        for copy in u_far:
            copy.wait_send()
        pl.semaphore_signal(turn, inc=1, device_id=at(zl_=1 - zl), device_id_type=MESH)
        pl.semaphore_wait(turn, 1)
        a_far[1].start()

    class Total:
        def __init__(self, call, sums, first, rows):
            self.call, self.sums, self.first, self.quarter = call, sums, first, rows // n_y

        def rows(self, y_, count=1):
            return pl.ds(pl.multiple_of(self.first + y_ * self.quarter, 8), count * self.quarter)

        def block(self, ref, slot):
            return ref.at[self.call, slot, pl.ds(0, self.sums), :, pl.ds(0, self.quarter)]

        def source(self, y_, count=1):
            return partial.at[pl.ds(0, self.sums), :, self.rows(y_, count)]

        def target(self, y_, count=1):
            return result.at[self.call, pl.ds(0, self.sums), :, self.rows(y_, count)]

        def wait(self, ref, sem, arrival):
            copy = pltpu.make_async_remote_copy(ref, ref, sem, sem, device_id=at(sibling), device_id_type=MESH)
            (copy.wait_recv if arrival else copy.wait_send)()

        def seven(self):
            return self.block(parts, pl.ds(1, 2 * n_y - 1))

        def gather(self, step):
            to = lax.rem(y + step, n_y)
            return pltpu.make_async_remote_copy(
                src_ref=self.source(to),
                dst_ref=self.block(parts, jnp.where(reducer, 0, n_y) + step),
                send_sem=in_send.at[self.call],
                recv_sem=in_recv.at[self.call],
                device_id=at(chip + zl, to),
                device_id_type=MESH,
            )

        def swap(self):
            return pltpu.make_async_remote_copy(
                src_ref=self.block(half_sum, slice(None)),
                dst_ref=self.block(half_in, slice(None)),
                send_sem=mid_send.at[self.call],
                recv_sem=mid_recv.at[self.call],
                device_id=at(sibling, zl_=1 - zl),
                device_id_type=MESH,
            )

        def spread(self, step, group):
            return pltpu.make_async_remote_copy(
                src_ref=self.block(total, group),
                dst_ref=self.target(y),
                send_sem=out_send.at[self.call],
                recv_sem=out_recv.at[self.call],
                device_id=at(sibling if group else gz, lax.rem(y + step, n_y)),
                device_id_type=MESH,
            )

        def send(self):
            for step in SPREAD:
                self.gather(step).start()

            @pl.when(jnp.logical_not(reducer))
            def _():
                self.gather(0).start()

        def reduce(self):
            @pl.when(reducer)
            def _():
                own = self.source(y)[...]
                self.wait(self.seven(), in_recv.at[self.call], True)
                for group in range(2):
                    block = self.block(parts, n_y)[...] if group else own
                    for step in range(1, n_y):
                        block = block + self.block(parts, group * n_y + step)[...]
                    self.block(half_sum, group)[...] = block
                self.swap().start()

        def finish(self):
            @pl.when(reducer)
            def _():
                self.swap().wait_recv()
                for group in range(2):
                    block = self.block(half_sum, group)[...] + self.block(half_in, 1 - group)[...]
                    self.block(total, group)[...] = block
                    if group == 0:
                        self.target(y)[...] = block
                for step in SPREAD:
                    for group in range(2):
                        self.spread(step, group).start()
                self.spread(0, 1).start()

        def arrive(self):
            for others, count in ((reducer, n_y - 1), (jnp.logical_not(reducer), n_y)):

                @pl.when(others)
                def _():
                    self.wait(self.target(0, count), out_recv.at[self.call], True)

        def drain(self):
            for others, count in ((reducer, n_y - 1), (jnp.logical_not(reducer), n_y)):

                @pl.when(others)
                def _():
                    self.wait(self.source(0, count), in_send.at[self.call], False)

            @pl.when(reducer)
            def _():
                self.swap().wait_send()
                self.wait(self.seven(), out_send.at[self.call], False)

    squares_first = Total(0, 1, 0, nx)
    second = [Total(1 + h, 2, h * half_rows, half_rows) for h in range(HALVES)]
    coupled_first = [Total(1 + HALVES + h, 1, h * half_rows, half_rows) for h in range(HALVES)]

    loads[0].wait()
    for z in range(planes):

        def add_square(p, acc):
            value = u[p, z]
            return acc + value * value

        partial[0, z] = lax.fori_loop(0, order, add_square, jnp.zeros((nx, ny), jnp.float32))
    squares_first.send()
    a_near.start()

    loads[2].wait()
    loads[3].wait()

    def own_middle(i, _):
        p, z = i // planes, lax.rem(i, planes)
        value = u[p, z]
        m, k = rate[p], stiff[p]
        slope = (1.0 + m) - (m * (1.0 - 2.0 * COUPLE)) * (value * value)
        mid[p, z] = value * slope + (m * k) * flat_laplacian(value, u[p, 1 - z])
        return 0

    lax.fori_loop(0, order * planes, own_middle, 0)
    loads[1].wait()

    def own_adjoint(i, _):
        p, z = i // planes, lax.rem(i, planes)
        value = a[p, z]
        m, k = rate[p], stiff[p]
        adj[p, z] = (1.0 + m) * value + (m * k) * flat_laplacian(value, a[p, 1 - z])
        return 0

    lax.fori_loop(0, order, own_adjoint, 0)
    squares_first.reduce()
    lax.fori_loop(order, order * planes, own_adjoint, 0)
    squares_first.finish()
    squares_first.arrive()
    squares_first.drain()

    def middle_half(h):
        rows = half(h)
        u_far[h].wait_recv()
        for z in range(planes):
            weight = (2.0 * COUPLE) * result[0, 0, z, rows]

            def middle(p, carry):
                squares, coupled = carry
                m, k = rate[p], stiff[p]
                value = mid[p, z, rows] - m * (u[p, z, rows] * weight)
                value = value + (m * k) * u_halo[p, z, rows]
                mid[p, z, rows] = value
                return squares + value * value, coupled + value * (m * a[p, z, rows])

            zero = jnp.zeros((half_rows, ny), jnp.float32)
            squares, coupled = lax.fori_loop(0, order, middle, (zero, zero))
            partial[0, z, rows] = squares
            partial[1, z, rows] = coupled
        second[h].send()

    def adjoint_half(h):
        rows = half(h)
        a_far[h].wait_recv()
        for z in range(planes):
            weight = (2.0 * COUPLE) * result[1 + h, 0, z, rows]
            pull = (4.0 * COUPLE) * result[1 + h, 1, z, rows]

            def adjoint(p, acc):
                m, k = rate[p], stiff[p]
                field = mid[p, z, rows]
                value = adj[p, z, rows] - (m * a[p, z, rows]) * (CUBE * (field * field) + weight)
                value = value - field * pull + (m * k) * a_halo[p, z, rows]
                adj[p, z, rows] = value
                scaled = m * value
                w[p, z, rows] = scaled
                return acc + u[p, z, rows] * scaled

            partial[0, z, rows] = lax.fori_loop(
                0, order, adjoint, jnp.zeros((half_rows, ny), jnp.float32)
            )
        w_far[h].start()
        w_near[h].start()
        coupled_first[h].send()

    u_near.wait_recv()
    middle_half(0)
    second[0].reduce()
    yield_link()
    middle_half(1)
    second[0].finish()
    second[1].reduce()
    second[0].arrive()
    second[0].drain()
    second[1].finish()
    a_near.wait_recv()
    adjoint_half(0)
    second[1].arrive()
    second[1].drain()
    coupled_first[0].reduce()
    adjoint_half(1)

    def own_result(i, _):
        p, z = i // planes, lax.rem(i, planes)
        value, scaled = u[p, z], w[p, z]
        slope = CUBE * (value * value) + (2.0 * COUPLE) * result[0, 0, z]
        local = adj[p, z] + scaled - scaled * slope
        adj[p, z] = local + stiff[p] * flat_laplacian(scaled, w[p, 1 - z])
        return 0

    coupled_first[0].finish()
    lax.fori_loop(0, order, own_result, 0)
    coupled_first[1].reduce()
    lax.fori_loop(order, order * planes, own_result, 0)
    coupled_first[1].finish()
    for h in range(HALVES):
        rows = half(h)
        coupled_first[h].arrive()
        for z in range(planes):
            pull = (4.0 * COUPLE) * result[1 + HALVES + h, 0, z, rows]

            def couple(p, _):
                adj[p, z, rows] = adj[p, z, rows] - u[p, z, rows] * pull
                return 0

            lax.fori_loop(0, order, couple, 0)
    store = pltpu.make_async_copy(adj, part, store_sem)
    store.start()
    for h in range(HALVES):
        coupled_first[h].drain()
    for copy in a_far + [u_near, a_near]:
        copy.wait_send()
    for copy in w_near + w_far:
        copy.wait()
    store.wait()


def on_device(n_gz, n_ord, initial, cotangent, mobility, stiffness):
    shape = initial.shape
    order, planes, nx, ny = shape
    n_y = n_ord // 2
    calls = 1 + 2 * HALVES
    f32 = jnp.float32
    field = jax.ShapeDtypeStruct(shape, f32)
    quarter = nx // n_y
    part, w_halo = pl.pallas_call(
        functools.partial(kernel, n_gz, n_y),
        out_shape=(field, field),
        in_specs=[pl.BlockSpec(memory_space=pltpu.HBM)] * 4,
        out_specs=[pl.BlockSpec(memory_space=pl.ANY)] * 2,
        scratch_shapes=[pltpu.SMEM((order,), f32)] * 2
        + [pltpu.VMEM(shape, f32)] * 7
        + [
            pltpu.VMEM((2, planes, nx, ny), f32),
            pltpu.VMEM((calls, 2 * n_y, 2, planes, quarter, ny), f32),
            pltpu.VMEM((calls, 2, 2, planes, quarter, ny), f32),
            pltpu.VMEM((calls, 2, 2, planes, quarter, ny), f32),
            pltpu.VMEM((calls, 2, 2, planes, quarter, ny), f32),
            pltpu.VMEM((calls, 2, planes, nx, ny), f32),
            pltpu.SemaphoreType.DMA((4,)),
            pltpu.SemaphoreType.DMA((3 * HALVES,)),
            pltpu.SemaphoreType.DMA((3 * HALVES,)),
            pltpu.SemaphoreType.DMA((2 + HALVES,)),
            pltpu.SemaphoreType.DMA((2 + HALVES,)),
        ]
        + [pltpu.SemaphoreType.DMA((calls,))] * 6
        + [
            pltpu.SemaphoreType.DMA,
            pltpu.SemaphoreType.REGULAR,
        ],
        compiler_params=pltpu.CompilerParams(
            collective_id=0, has_side_effects=True, vmem_limit_bytes=32 << 20
        ),
        name="adjoint_steps",
    )(*(pltpu.with_memory_space_constraint(x, pltpu.HBM) for x in (initial, cotangent, mobility, stiffness)))
    return part + stiffness.reshape(-1, 1, 1, 1) * w_halo


def solution(mesh):
    return jax.shard_map(
        functools.partial(on_device, mesh.shape["gz"], mesh.shape["ord"]),
        mesh=mesh,
        in_specs=(P("ord", "gz", None, None), P("ord", "gz", None, None), P("ord"), P("ord")),
        out_specs=P("ord", "gz", None, None),
        check_vma=False,
    )
```

```python
import functools

import jax
import jax.numpy as jnp
from jax import lax
from jax.experimental import pallas as pl
from jax.experimental.pallas import tpu as pltpu
from jax.sharding import PartitionSpec as P

P_SIZE = 96
COUPLE = 2.0 / P_SIZE
CUBE = 3.0 - 6.0 * COUPLE
MESH = pl.DeviceIdType.MESH
HALVES = 2
SPREAD = (2, 1, 3)


def flat_laplacian(plane, other):
    rows, cols = plane.shape
    side = pltpu.roll(plane, 1, 0) + pltpu.roll(plane, rows - 1, 0)
    side = side + (pltpu.roll(plane, 1, 1) + pltpu.roll(plane, cols - 1, 1))
    return side + (other - 6.0 * plane)


def kernel(
    n_gz, n_y,
    u_hbm, a_hbm, rate_hbm, stiff_hbm,
    part, w_halo,
    rate, stiff, u, a, mid, adj, w, u_halo, a_halo, partial, parts, half_sum, half_in, total, result,
    load_sem, far_send, far_recv, near_send, near_recv,
    in_send, in_recv, mid_send, mid_recv, out_send, out_recv, store_sem, turn,
):
    order, planes, nx, ny = u.shape
    gz, ord_ = lax.axis_index("gz"), lax.axis_index("ord")
    core, y, zl = lax.rem(gz, 2), ord_ // 2, lax.rem(ord_, 2)
    sibling = gz + 1 - 2 * core
    chip = gz - core
    far = lax.rem(jnp.where(core == 1, gz + 1, gz + n_gz - 1), n_gz)
    far_plane, near_plane = core, 1 - core
    reducer = core == zl
    half_rows = nx // HALVES

    def at(gz_=None, y_=None, zl_=None):
        y_ = y if y_ is None else y_
        zl_ = zl if zl_ is None else zl_
        return {"gz": gz if gz_ is None else gz_, "ord": 2 * y_ + zl_}

    loads = [
        pltpu.make_async_copy(u_hbm, u, load_sem.at[0]),
        pltpu.make_async_copy(a_hbm, a, load_sem.at[1]),
        pltpu.make_async_copy(rate_hbm, rate, load_sem.at[2]),
        pltpu.make_async_copy(stiff_hbm, stiff, load_sem.at[3]),
    ]
    for copy in loads:
        copy.start()

    barrier = pltpu.get_barrier_semaphore()
    peers = [at(far), at(sibling, zl_=1 - zl), at(sibling), at(zl_=1 - zl)]
    for step in range(1, n_y):
        for c in range(2):
            peers.append(at(chip + c, lax.rem(y + step, n_y)))
    for peer in peers:
        pl.semaphore_signal(barrier, inc=1, device_id=peer, device_id_type=MESH)
    pl.semaphore_wait(barrier, len(peers))

    def halo(index, src, dst, far_side, rows):
        mine = far_plane if far_side else near_plane
        theirs = 1 - mine
        return pltpu.make_async_remote_copy(
            src_ref=src.at[:, mine, rows],
            dst_ref=dst.at[:, theirs, rows],
            send_sem=(far_send if far_side else near_send).at[index],
            recv_sem=(far_recv if far_side else near_recv).at[index],
            device_id=at(far if far_side else sibling),
            device_id_type=MESH,
        )

    def half(h):
        return pl.ds(h * half_rows, half_rows)

    u_far = [halo(h, u_hbm, u_halo, True, half(h)) for h in range(HALVES)]
    a_far = [halo(HALVES + h, a_hbm, a_halo, True, half(h)) for h in range(HALVES)]
    w_far = [halo(2 * HALVES + h, w, w_halo, True, half(h)) for h in range(HALVES)]
    u_near = halo(0, u_hbm, u_halo, False, pl.ds(0, nx))
    a_near = halo(1, a_hbm, a_halo, False, pl.ds(0, nx))
    w_near = [halo(2 + h, w, w_halo, False, half(h)) for h in range(HALVES)]
    for copy in u_far + [u_near]:
        copy.start()

    a_far[0].start()

    def yield_link():
        for copy in u_far:
            copy.wait_send()
        pl.semaphore_signal(turn, inc=1, device_id=at(zl_=1 - zl), device_id_type=MESH)
        pl.semaphore_wait(turn, 1)
        a_far[1].start()

    class Total:
        def __init__(self, call, sums, first, rows):
            self.call, self.sums, self.first, self.quarter = call, sums, first, rows // n_y

        def rows(self, y_, count=1):
            return pl.ds(pl.multiple_of(self.first + y_ * self.quarter, 8), count * self.quarter)

        def block(self, ref, slot):
            return ref.at[self.call, slot, pl.ds(0, self.sums), :, pl.ds(0, self.quarter)]

        def source(self, y_, count=1):
            return partial.at[pl.ds(0, self.sums), :, self.rows(y_, count)]

        def target(self, y_, count=1):
            return result.at[self.call, pl.ds(0, self.sums), :, self.rows(y_, count)]

        def wait(self, ref, sem, arrival):
            copy = pltpu.make_async_remote_copy(ref, ref, sem, sem, device_id=at(sibling), device_id_type=MESH)
            (copy.wait_recv if arrival else copy.wait_send)()

        def seven(self):
            return self.block(parts, pl.ds(1, 2 * n_y - 1))

        def gather(self, step):
            to = lax.rem(y + step, n_y)
            return pltpu.make_async_remote_copy(
                src_ref=self.source(to),
                dst_ref=self.block(parts, jnp.where(reducer, 0, n_y) + step),
                send_sem=in_send.at[self.call],
                recv_sem=in_recv.at[self.call],
                device_id=at(chip + zl, to),
                device_id_type=MESH,
            )

        def swap(self):
            return pltpu.make_async_remote_copy(
                src_ref=self.block(half_sum, slice(None)),
                dst_ref=self.block(half_in, slice(None)),
                send_sem=mid_send.at[self.call],
                recv_sem=mid_recv.at[self.call],
                device_id=at(sibling, zl_=1 - zl),
                device_id_type=MESH,
            )

        def spread(self, step, group):
            return pltpu.make_async_remote_copy(
                src_ref=self.block(total, group),
                dst_ref=self.target(y),
                send_sem=out_send.at[self.call],
                recv_sem=out_recv.at[self.call],
                device_id=at(sibling if group else gz, lax.rem(y + step, n_y)),
                device_id_type=MESH,
            )

        def send(self):
            for step in SPREAD:
                self.gather(step).start()

            @pl.when(jnp.logical_not(reducer))
            def _():
                self.gather(0).start()

        def reduce(self):
            @pl.when(reducer)
            def _():
                own = self.source(y)[...]
                self.wait(self.seven(), in_recv.at[self.call], True)
                for group in range(2):
                    block = self.block(parts, n_y)[...] if group else own
                    for step in range(1, n_y):
                        block = block + self.block(parts, group * n_y + step)[...]
                    self.block(half_sum, group)[...] = block
                self.swap().start()

        def finish(self):
            @pl.when(reducer)
            def _():
                self.swap().wait_recv()
                for group in range(2):
                    block = self.block(half_sum, group)[...] + self.block(half_in, 1 - group)[...]
                    self.block(total, group)[...] = block
                    if group == 0:
                        self.target(y)[...] = block
                for step in SPREAD:
                    for group in range(2):
                        self.spread(step, group).start()
                self.spread(0, 1).start()

        def arrive(self):
            for others, count in ((reducer, n_y - 1), (jnp.logical_not(reducer), n_y)):

                @pl.when(others)
                def _():
                    self.wait(self.target(0, count), out_recv.at[self.call], True)

        def drain(self):
            for others, count in ((reducer, n_y - 1), (jnp.logical_not(reducer), n_y)):

                @pl.when(others)
                def _():
                    self.wait(self.source(0, count), in_send.at[self.call], False)

            @pl.when(reducer)
            def _():
                self.swap().wait_send()
                self.wait(self.seven(), out_send.at[self.call], False)

    squares_first = Total(0, 1, 0, nx)
    second = [Total(1 + h, 2, h * half_rows, half_rows) for h in range(HALVES)]
    coupled_first = [Total(1 + HALVES + h, 1, h * half_rows, half_rows) for h in range(HALVES)]

    loads[0].wait()
    for z in range(planes):

        def add_square(p, acc):
            value = u[p, z]
            return acc + value * value

        partial[0, z] = lax.fori_loop(0, order, add_square, jnp.zeros((nx, ny), jnp.float32))
    squares_first.send()
    a_near.start()

    loads[2].wait()
    loads[3].wait()

    def own_middle(i, _):
        p, z = i // planes, lax.rem(i, planes)
        value = u[p, z]
        m, k = rate[p], stiff[p]
        slope = (1.0 + m) - (m * (1.0 - 2.0 * COUPLE)) * (value * value)
        mid[p, z] = value * slope + (m * k) * flat_laplacian(value, u[p, 1 - z])
        return 0

    lax.fori_loop(0, order * planes, own_middle, 0)
    loads[1].wait()

    def own_adjoint(i, _):
        p, z = i // planes, lax.rem(i, planes)
        value = a[p, z]
        m, k = rate[p], stiff[p]
        adj[p, z] = (1.0 + m) * value + (m * k) * flat_laplacian(value, a[p, 1 - z])
        return 0

    lax.fori_loop(0, order, own_adjoint, 0)
    squares_first.reduce()
    lax.fori_loop(order, order * planes, own_adjoint, 0)
    squares_first.finish()
    squares_first.arrive()
    squares_first.drain()

    def middle_half(h):
        rows = half(h)
        u_far[h].wait_recv()
        for z in range(planes):
            weight = (2.0 * COUPLE) * result[0, 0, z, rows]

            def middle(p, carry):
                squares, coupled = carry
                m, k = rate[p], stiff[p]
                value = mid[p, z, rows] - m * (u[p, z, rows] * weight)
                value = value + (m * k) * u_halo[p, z, rows]
                mid[p, z, rows] = value
                return squares + value * value, coupled + value * (m * a[p, z, rows])

            zero = jnp.zeros((half_rows, ny), jnp.float32)
            squares, coupled = lax.fori_loop(0, order, middle, (zero, zero))
            partial[0, z, rows] = squares
            partial[1, z, rows] = coupled
        second[h].send()

    def adjoint_half(h):
        rows = half(h)
        a_far[h].wait_recv()
        for z in range(planes):
            weight = (2.0 * COUPLE) * result[1 + h, 0, z, rows]
            pull = (4.0 * COUPLE) * result[1 + h, 1, z, rows]

            def adjoint(p, acc):
                m, k = rate[p], stiff[p]
                field = mid[p, z, rows]
                value = adj[p, z, rows] - (m * a[p, z, rows]) * (CUBE * (field * field) + weight)
                value = value - field * pull + (m * k) * a_halo[p, z, rows]
                adj[p, z, rows] = value
                scaled = m * value
                w[p, z, rows] = k * scaled
                return acc + u[p, z, rows] * scaled

            partial[0, z, rows] = lax.fori_loop(
                0, order, adjoint, jnp.zeros((half_rows, ny), jnp.float32)
            )
        w_far[h].start()
        w_near[h].start()
        coupled_first[h].send()

    u_near.wait_recv()
    middle_half(0)
    second[0].reduce()
    yield_link()
    middle_half(1)
    second[0].finish()
    second[1].reduce()
    second[0].arrive()
    second[0].drain()
    second[1].finish()
    a_near.wait_recv()
    adjoint_half(0)
    second[1].arrive()
    second[1].drain()
    adjoint_half(1)
    coupled_first[0].reduce()

    def own_result(i, _):
        p, z = i // planes, lax.rem(i, planes)
        value, full = u[p, z], adj[p, z]
        slope = CUBE * (value * value) + (2.0 * COUPLE) * result[0, 0, z]
        local = full + (rate[p] * full) * (1.0 - slope)
        adj[p, z] = local + flat_laplacian(w[p, z], w[p, 1 - z])
        return 0

    lax.fori_loop(0, order * planes, own_result, 0)
    coupled_first[1].reduce()
    coupled_first[0].finish()
    coupled_first[1].finish()
    for h in range(HALVES):
        rows = half(h)
        coupled_first[h].arrive()
        for z in range(planes):
            pull = (4.0 * COUPLE) * result[1 + HALVES + h, 0, z, rows]

            def couple(p, _):
                adj[p, z, rows] = adj[p, z, rows] - u[p, z, rows] * pull
                return 0

            lax.fori_loop(0, order, couple, 0)
    store = pltpu.make_async_copy(adj, part, store_sem)
    store.start()
    for h in range(HALVES):
        coupled_first[h].drain()
    for copy in a_far + [u_near, a_near]:
        copy.wait_send()
    for copy in w_near + w_far:
        copy.wait()
    store.wait()


def add_halo(part, w_halo, out, whole, sem):
    order = whole.shape[0]

    def one(p, _):
        whole[p] = part[p] + w_halo[p]
        pltpu.make_async_copy(whole.at[p], out.at[p], sem).start()
        return 0

    lax.fori_loop(0, order, one, 0)
    pltpu.make_async_copy(whole, out, sem).wait()


def on_device(n_gz, n_ord, initial, cotangent, mobility, stiffness):
    shape = initial.shape
    order, planes, nx, ny = shape
    n_y = n_ord // 2
    calls = 1 + 2 * HALVES
    f32 = jnp.float32
    field = jax.ShapeDtypeStruct(shape, f32)
    quarter = nx // n_y
    part, w_halo = pl.pallas_call(
        functools.partial(kernel, n_gz, n_y),
        out_shape=(field, field),
        in_specs=[pl.BlockSpec(memory_space=pltpu.HBM)] * 4,
        out_specs=[pl.BlockSpec(memory_space=pl.ANY)] * 2,
        scratch_shapes=[pltpu.SMEM((order,), f32)] * 2
        + [pltpu.VMEM(shape, f32)] * 7
        + [
            pltpu.VMEM((2, planes, nx, ny), f32),
            pltpu.VMEM((calls, 2 * n_y, 2, planes, quarter, ny), f32),
            pltpu.VMEM((calls, 2, 2, planes, quarter, ny), f32),
            pltpu.VMEM((calls, 2, 2, planes, quarter, ny), f32),
            pltpu.VMEM((calls, 2, 2, planes, quarter, ny), f32),
            pltpu.VMEM((calls, 2, planes, nx, ny), f32),
            pltpu.SemaphoreType.DMA((4,)),
            pltpu.SemaphoreType.DMA((3 * HALVES,)),
            pltpu.SemaphoreType.DMA((3 * HALVES,)),
            pltpu.SemaphoreType.DMA((2 + HALVES,)),
            pltpu.SemaphoreType.DMA((2 + HALVES,)),
        ]
        + [pltpu.SemaphoreType.DMA((calls,))] * 6
        + [
            pltpu.SemaphoreType.DMA,
            pltpu.SemaphoreType.REGULAR,
        ],
        compiler_params=pltpu.CompilerParams(
            collective_id=0, has_side_effects=True, vmem_limit_bytes=32 << 20
        ),
        name="adjoint_steps",
    )(*(pltpu.with_memory_space_constraint(x, pltpu.HBM) for x in (initial, cotangent, mobility, stiffness)))
    return pl.pallas_call(
        add_halo,
        out_shape=field,
        in_specs=[pl.BlockSpec(memory_space=pltpu.VMEM)] * 2,
        out_specs=pl.BlockSpec(memory_space=pltpu.HBM),
        scratch_shapes=[pltpu.VMEM(shape, f32), pltpu.SemaphoreType.DMA],
        compiler_params=pltpu.CompilerParams(vmem_limit_bytes=16 << 20),
        name="add_halo",
    )(part, w_halo)


def solution(mesh):
    return jax.shard_map(
        functools.partial(on_device, mesh.shape["gz"], mesh.shape["ord"]),
        mesh=mesh,
        in_specs=(P("ord", "gz", None, None), P("ord", "gz", None, None), P("ord"), P("ord")),
        out_specs=P("ord", "gz", None, None),
        check_vma=False,
    )
```

```python
import functools

import jax
import jax.numpy as jnp
from jax import lax
from jax.experimental import pallas as pl
from jax.experimental.pallas import tpu as pltpu
from jax.sharding import PartitionSpec as P

P_SIZE = 96
COUPLE = 2.0 / P_SIZE
CUBE = 3.0 - 6.0 * COUPLE
MESH = pl.DeviceIdType.MESH
HALVES = 2
SPREAD = (2, 1, 3)


def flat_laplacian(plane, other):
    rows, cols = plane.shape
    side = pltpu.roll(plane, 1, 0) + pltpu.roll(plane, rows - 1, 0)
    side = side + (pltpu.roll(plane, 1, 1) + pltpu.roll(plane, cols - 1, 1))
    return side + (other - 6.0 * plane)


def kernel(
    n_gz, n_y,
    u_hbm, a_hbm, rate_hbm, stiff_hbm,
    part, w_halo,
    rate, stiff, u, a, mid, adj, w, u_halo, a_halo, partial, parts, half_sum, half_in, total, result,
    load_sem, far_send, far_recv, near_send, near_recv,
    in_send, in_recv, mid_send, mid_recv, out_send, out_recv, store_sem, turn,
):
    order, planes, nx, ny = u.shape
    gz, ord_ = lax.axis_index("gz"), lax.axis_index("ord")
    core, y, zl = lax.rem(gz, 2), ord_ // 2, lax.rem(ord_, 2)
    sibling = gz + 1 - 2 * core
    chip = gz - core
    far = lax.rem(jnp.where(core == 1, gz + 1, gz + n_gz - 1), n_gz)
    far_plane, near_plane = core, 1 - core
    reducer = core == zl
    half_rows = nx // HALVES

    def at(gz_=None, y_=None, zl_=None):
        y_ = y if y_ is None else y_
        zl_ = zl if zl_ is None else zl_
        return {"gz": gz if gz_ is None else gz_, "ord": 2 * y_ + zl_}

    loads = [
        pltpu.make_async_copy(u_hbm, u, load_sem.at[0]),
        pltpu.make_async_copy(a_hbm, a, load_sem.at[1]),
        pltpu.make_async_copy(rate_hbm, rate, load_sem.at[2]),
        pltpu.make_async_copy(stiff_hbm, stiff, load_sem.at[3]),
    ]
    for copy in loads:
        copy.start()

    barrier = pltpu.get_barrier_semaphore()
    peers = [at(far), at(sibling, zl_=1 - zl), at(sibling), at(zl_=1 - zl)]
    for step in range(1, n_y):
        for c in range(2):
            peers.append(at(chip + c, lax.rem(y + step, n_y)))
    for peer in peers:
        pl.semaphore_signal(barrier, inc=1, device_id=peer, device_id_type=MESH)
    pl.semaphore_wait(barrier, len(peers))

    def halo(index, src, dst, far_side, rows):
        mine = far_plane if far_side else near_plane
        theirs = 1 - mine
        return pltpu.make_async_remote_copy(
            src_ref=src.at[:, mine, rows],
            dst_ref=dst.at[:, theirs, rows],
            send_sem=(far_send if far_side else near_send).at[index],
            recv_sem=(far_recv if far_side else near_recv).at[index],
            device_id=at(far if far_side else sibling),
            device_id_type=MESH,
        )

    def half(h):
        return pl.ds(h * half_rows, half_rows)

    u_far = [halo(h, u_hbm, u_halo, True, half(h)) for h in range(HALVES)]
    a_far = [halo(HALVES + h, a_hbm, a_halo, True, half(h)) for h in range(HALVES)]
    w_far = [halo(2 * HALVES + h, w, w_halo, True, half(h)) for h in range(HALVES)]
    u_near = halo(0, u_hbm, u_halo, False, pl.ds(0, nx))
    a_near = halo(1, a_hbm, a_halo, False, pl.ds(0, nx))
    w_near = [halo(2 + h, w, w_halo, False, half(h)) for h in range(HALVES)]
    for copy in u_far + [u_near]:
        copy.start()

    a_far[0].start()

    def yield_link():
        for copy in u_far:
            copy.wait_send()
        pl.semaphore_signal(turn, inc=1, device_id=at(zl_=1 - zl), device_id_type=MESH)
        pl.semaphore_wait(turn, 1)
        a_far[1].start()

    class Total:
        def __init__(self, call, sums, first, rows):
            self.call, self.sums, self.first, self.quarter = call, sums, first, rows // n_y

        def rows(self, y_, count=1):
            return pl.ds(pl.multiple_of(self.first + y_ * self.quarter, 8), count * self.quarter)

        def block(self, ref, slot):
            return ref.at[self.call, slot, pl.ds(0, self.sums), :, pl.ds(0, self.quarter)]

        def source(self, y_, count=1):
            return partial.at[pl.ds(0, self.sums), :, self.rows(y_, count)]

        def target(self, y_, count=1):
            return result.at[self.call, pl.ds(0, self.sums), :, self.rows(y_, count)]

        def wait(self, ref, sem, arrival):
            copy = pltpu.make_async_remote_copy(ref, ref, sem, sem, device_id=at(sibling), device_id_type=MESH)
            (copy.wait_recv if arrival else copy.wait_send)()

        def seven(self):
            return self.block(parts, pl.ds(1, 2 * n_y - 1))

        def gather(self, step):
            to = lax.rem(y + step, n_y)
            return pltpu.make_async_remote_copy(
                src_ref=self.source(to),
                dst_ref=self.block(parts, jnp.where(reducer, 0, n_y) + step),
                send_sem=in_send.at[self.call],
                recv_sem=in_recv.at[self.call],
                device_id=at(chip + zl, to),
                device_id_type=MESH,
            )

        def swap(self):
            return pltpu.make_async_remote_copy(
                src_ref=self.block(half_sum, slice(None)),
                dst_ref=self.block(half_in, slice(None)),
                send_sem=mid_send.at[self.call],
                recv_sem=mid_recv.at[self.call],
                device_id=at(sibling, zl_=1 - zl),
                device_id_type=MESH,
            )

        def spread(self, step, group):
            return pltpu.make_async_remote_copy(
                src_ref=self.block(total, group),
                dst_ref=self.target(y),
                send_sem=out_send.at[self.call],
                recv_sem=out_recv.at[self.call],
                device_id=at(sibling if group else gz, lax.rem(y + step, n_y)),
                device_id_type=MESH,
            )

        def send(self):
            for step in SPREAD:
                self.gather(step).start()

            @pl.when(jnp.logical_not(reducer))
            def _():
                self.gather(0).start()

        def reduce(self):
            @pl.when(reducer)
            def _():
                own = self.source(y)[...]
                self.wait(self.seven(), in_recv.at[self.call], True)
                for group in range(2):
                    block = self.block(parts, n_y)[...] if group else own
                    for step in range(1, n_y):
                        block = block + self.block(parts, group * n_y + step)[...]
                    self.block(half_sum, group)[...] = block
                self.swap().start()

        def finish(self):
            @pl.when(reducer)
            def _():
                self.swap().wait_recv()
                for group in range(2):
                    block = self.block(half_sum, group)[...] + self.block(half_in, 1 - group)[...]
                    self.block(total, group)[...] = block
                    if group == 0:
                        self.target(y)[...] = block
                for step in SPREAD:
                    for group in range(2):
                        self.spread(step, group).start()
                self.spread(0, 1).start()

        def arrive(self):
            for others, count in ((reducer, n_y - 1), (jnp.logical_not(reducer), n_y)):

                @pl.when(others)
                def _():
                    self.wait(self.target(0, count), out_recv.at[self.call], True)

        def drain(self):
            for others, count in ((reducer, n_y - 1), (jnp.logical_not(reducer), n_y)):

                @pl.when(others)
                def _():
                    self.wait(self.source(0, count), in_send.at[self.call], False)

            @pl.when(reducer)
            def _():
                self.swap().wait_send()
                self.wait(self.seven(), out_send.at[self.call], False)

    squares_first = Total(0, 1, 0, nx)
    second = [Total(1 + h, 2, h * half_rows, half_rows) for h in range(HALVES)]
    coupled_first = [Total(1 + HALVES + h, 1, h * half_rows, half_rows) for h in range(HALVES)]

    loads[0].wait()
    for z in range(planes):

        def add_square(p, acc):
            value = u[p, z]
            return acc + value * value

        partial[0, z] = lax.fori_loop(0, order, add_square, jnp.zeros((nx, ny), jnp.float32))
    squares_first.send()
    a_near.start()

    loads[2].wait()
    loads[3].wait()

    def own_middle(i, _):
        p, z = i // planes, lax.rem(i, planes)
        value = u[p, z]
        m, k = rate[p], stiff[p]
        slope = (1.0 + m) - (m * (1.0 - 2.0 * COUPLE)) * (value * value)
        mid[p, z] = value * slope + (m * k) * flat_laplacian(value, u[p, 1 - z])
        return 0

    lax.fori_loop(0, order * planes, own_middle, 0)
    loads[1].wait()

    def own_adjoint(i, _):
        p, z = i // planes, lax.rem(i, planes)
        value = a[p, z]
        m, k = rate[p], stiff[p]
        adj[p, z] = (1.0 + m) * value + (m * k) * flat_laplacian(value, a[p, 1 - z])
        return 0

    lax.fori_loop(0, order, own_adjoint, 0)
    squares_first.reduce()
    lax.fori_loop(order, order * planes, own_adjoint, 0)
    squares_first.finish()
    squares_first.arrive()
    squares_first.drain()

    def middle_half(h):
        rows = half(h)
        u_far[h].wait_recv()
        for z in range(planes):
            weight = (2.0 * COUPLE) * result[0, 0, z, rows]

            def middle(p, carry):
                squares, coupled = carry
                m, k = rate[p], stiff[p]
                value = mid[p, z, rows] - m * (u[p, z, rows] * weight)
                value = value + (m * k) * u_halo[p, z, rows]
                mid[p, z, rows] = value
                return squares + value * value, coupled + value * (m * a[p, z, rows])

            zero = jnp.zeros((half_rows, ny), jnp.float32)
            squares, coupled = lax.fori_loop(0, order, middle, (zero, zero))
            partial[0, z, rows] = squares
            partial[1, z, rows] = coupled
        second[h].send()

    def adjoint_half(h):
        rows = half(h)
        a_far[h].wait_recv()
        for z in range(planes):
            weight = (2.0 * COUPLE) * result[1 + h, 0, z, rows]
            pull = (4.0 * COUPLE) * result[1 + h, 1, z, rows]

            def adjoint(p, acc):
                m, k = rate[p], stiff[p]
                field = mid[p, z, rows]
                value = adj[p, z, rows] - (m * a[p, z, rows]) * (CUBE * (field * field) + weight)
                value = value - field * pull + (m * k) * a_halo[p, z, rows]
                adj[p, z, rows] = value
                scaled = m * value
                w[p, z, rows] = k * scaled
                return acc + u[p, z, rows] * scaled

            partial[0, z, rows] = lax.fori_loop(
                0, order, adjoint, jnp.zeros((half_rows, ny), jnp.float32)
            )
        if h == 0:
            w_far[0].start()
        else:
            pl.when(jnp.logical_not(reducer))(w_far[1].start)
        w_near[h].start()
        coupled_first[h].send()

    u_near.wait_recv()
    middle_half(0)
    second[0].reduce()
    yield_link()
    middle_half(1)
    second[0].finish()
    second[1].reduce()
    second[0].arrive()
    second[0].drain()
    second[1].finish()
    a_near.wait_recv()
    adjoint_half(0)
    second[1].arrive()
    second[1].drain()
    adjoint_half(1)
    coupled_first[0].reduce()

    def own_result(i, _):
        p, z = i // planes, lax.rem(i, planes)
        value, full = u[p, z], adj[p, z]
        slope = CUBE * (value * value) + (2.0 * COUPLE) * result[0, 0, z]
        local = full + (rate[p] * full) * (1.0 - slope)
        adj[p, z] = local + flat_laplacian(w[p, z], w[p, 1 - z])
        return 0

    lax.fori_loop(0, order * planes, own_result, 0)
    coupled_first[1].reduce()

    @pl.when(reducer)
    def _():
        pl.semaphore_wait(turn, 1)
        w_far[1].start()

    @pl.when(jnp.logical_not(reducer))
    def _():
        w_far[0].wait_send()
        pl.semaphore_signal(turn, inc=1, device_id=at(zl_=1 - zl), device_id_type=MESH)

    coupled_first[0].finish()
    coupled_first[1].finish()
    for h in range(HALVES):
        rows = half(h)
        coupled_first[h].arrive()
        for z in range(planes):
            pull = (4.0 * COUPLE) * result[1 + HALVES + h, 0, z, rows]

            def couple(p, _):
                adj[p, z, rows] = adj[p, z, rows] - u[p, z, rows] * pull
                return 0

            lax.fori_loop(0, order, couple, 0)
    store = pltpu.make_async_copy(adj, part, store_sem)
    store.start()
    for h in range(HALVES):
        coupled_first[h].drain()
    for copy in a_far + [u_near, a_near]:
        copy.wait_send()
    for copy in w_near + [w_far[1]]:
        copy.wait()
    w_far[0].wait_recv()

    @pl.when(reducer)
    def _():
        w_far[0].wait_send()
    store.wait()


def add_halo(part, w_halo, out, whole, sem):
    order = whole.shape[0]

    def one(p, _):
        whole[p] = part[p] + w_halo[p]
        pltpu.make_async_copy(whole.at[p], out.at[p], sem).start()
        return 0

    lax.fori_loop(0, order, one, 0)
    pltpu.make_async_copy(whole, out, sem).wait()


def on_device(n_gz, n_ord, initial, cotangent, mobility, stiffness):
    shape = initial.shape
    order, planes, nx, ny = shape
    n_y = n_ord // 2
    calls = 1 + 2 * HALVES
    f32 = jnp.float32
    field = jax.ShapeDtypeStruct(shape, f32)
    quarter = nx // n_y
    part, w_halo = pl.pallas_call(
        functools.partial(kernel, n_gz, n_y),
        out_shape=(field, field),
        in_specs=[pl.BlockSpec(memory_space=pltpu.HBM)] * 4,
        out_specs=[pl.BlockSpec(memory_space=pl.ANY)] * 2,
        scratch_shapes=[pltpu.SMEM((order,), f32)] * 2
        + [pltpu.VMEM(shape, f32)] * 7
        + [
            pltpu.VMEM((2, planes, nx, ny), f32),
            pltpu.VMEM((calls, 2 * n_y, 2, planes, quarter, ny), f32),
            pltpu.VMEM((calls, 2, 2, planes, quarter, ny), f32),
            pltpu.VMEM((calls, 2, 2, planes, quarter, ny), f32),
            pltpu.VMEM((calls, 2, 2, planes, quarter, ny), f32),
            pltpu.VMEM((calls, 2, planes, nx, ny), f32),
            pltpu.SemaphoreType.DMA((4,)),
            pltpu.SemaphoreType.DMA((3 * HALVES,)),
            pltpu.SemaphoreType.DMA((3 * HALVES,)),
            pltpu.SemaphoreType.DMA((2 + HALVES,)),
            pltpu.SemaphoreType.DMA((2 + HALVES,)),
        ]
        + [pltpu.SemaphoreType.DMA((calls,))] * 6
        + [
            pltpu.SemaphoreType.DMA,
            pltpu.SemaphoreType.REGULAR,
        ],
        compiler_params=pltpu.CompilerParams(
            collective_id=0, has_side_effects=True, vmem_limit_bytes=32 << 20
        ),
        name="adjoint_steps",
    )(*(pltpu.with_memory_space_constraint(x, pltpu.HBM) for x in (initial, cotangent, mobility, stiffness)))
    return pl.pallas_call(
        add_halo,
        out_shape=field,
        in_specs=[pl.BlockSpec(memory_space=pltpu.VMEM)] * 2,
        out_specs=pl.BlockSpec(memory_space=pltpu.HBM),
        scratch_shapes=[pltpu.VMEM(shape, f32), pltpu.SemaphoreType.DMA],
        compiler_params=pltpu.CompilerParams(vmem_limit_bytes=16 << 20),
        name="add_halo",
    )(part, w_halo)


def solution(mesh):
    return jax.shard_map(
        functools.partial(on_device, mesh.shape["gz"], mesh.shape["ord"]),
        mesh=mesh,
        in_specs=(P("ord", "gz", None, None), P("ord", "gz", None, None), P("ord"), P("ord")),
        out_specs=P("ord", "gz", None, None),
        check_vma=False,
    )
```

```python
import functools

import jax
import jax.numpy as jnp
from jax import lax
from jax.experimental import pallas as pl
from jax.experimental.pallas import tpu as pltpu
from jax.sharding import PartitionSpec as P

P_SIZE = 96
COUPLE = 2.0 / P_SIZE
CUBE = 3.0 - 6.0 * COUPLE
MESH = pl.DeviceIdType.MESH
HALVES = 2
SPREAD = (2, 1, 3)


def flat_laplacian(plane, other):
    rows, cols = plane.shape
    side = pltpu.roll(plane, 1, 0) + pltpu.roll(plane, rows - 1, 0)
    side = side + (pltpu.roll(plane, 1, 1) + pltpu.roll(plane, cols - 1, 1))
    return side + (other - 6.0 * plane)


def kernel(
    n_gz, n_y,
    u_hbm, a_hbm, rate_hbm, stiff_hbm,
    part, w_halo,
    rate, stiff, u, a, mid, adj, w, u_halo, a_halo, partial, parts, half_sum, half_in, total, result,
    load_sem, far_send, far_recv, near_send, near_recv,
    in_send, in_recv, mid_send, mid_recv, out_send, out_recv, store_sem, turn,
):
    order, planes, nx, ny = u.shape
    gz, ord_ = lax.axis_index("gz"), lax.axis_index("ord")
    core, y, zl = lax.rem(gz, 2), ord_ // 2, lax.rem(ord_, 2)
    sibling = gz + 1 - 2 * core
    chip = gz - core
    far = lax.rem(jnp.where(core == 1, gz + 1, gz + n_gz - 1), n_gz)
    far_plane, near_plane = core, 1 - core
    reducer = core == zl
    half_rows = nx // HALVES

    def at(gz_=None, y_=None, zl_=None):
        y_ = y if y_ is None else y_
        zl_ = zl if zl_ is None else zl_
        return {"gz": gz if gz_ is None else gz_, "ord": 2 * y_ + zl_}

    loads = [
        pltpu.make_async_copy(u_hbm, u, load_sem.at[0]),
        pltpu.make_async_copy(a_hbm, a, load_sem.at[1]),
        pltpu.make_async_copy(rate_hbm, rate, load_sem.at[2]),
        pltpu.make_async_copy(stiff_hbm, stiff, load_sem.at[3]),
    ]
    for copy in loads:
        copy.start()

    barrier = pltpu.get_barrier_semaphore()
    peers = [at(far), at(sibling, zl_=1 - zl), at(sibling), at(zl_=1 - zl)]
    for step in range(1, n_y):
        for c in range(2):
            peers.append(at(chip + c, lax.rem(y + step, n_y)))
    for peer in peers:
        pl.semaphore_signal(barrier, inc=1, device_id=peer, device_id_type=MESH)
    pl.semaphore_wait(barrier, len(peers))

    def halo(index, src, dst, far_side, rows):
        mine = far_plane if far_side else near_plane
        theirs = 1 - mine
        return pltpu.make_async_remote_copy(
            src_ref=src.at[:, mine, rows],
            dst_ref=dst.at[:, theirs, rows],
            send_sem=(far_send if far_side else near_send).at[index],
            recv_sem=(far_recv if far_side else near_recv).at[index],
            device_id=at(far if far_side else sibling),
            device_id_type=MESH,
        )

    def half(h):
        return pl.ds(h * half_rows, half_rows)

    u_far = [halo(h, u_hbm, u_halo, True, half(h)) for h in range(HALVES)]
    a_far = [halo(HALVES + h, a_hbm, a_halo, True, half(h)) for h in range(HALVES)]
    w_far = [halo(2 * HALVES + h, w, w_halo, True, half(h)) for h in range(HALVES)]
    u_near = halo(0, u_hbm, u_halo, False, pl.ds(0, nx))
    a_near = halo(1, a_hbm, a_halo, False, pl.ds(0, nx))
    w_near = [halo(2 + h, w, w_halo, False, half(h)) for h in range(HALVES)]
    for copy in u_far + [u_near]:
        copy.start()

    a_far[0].start()

    def yield_link():
        for copy in u_far:
            copy.wait_send()
        pl.semaphore_signal(turn, inc=1, device_id=at(zl_=1 - zl), device_id_type=MESH)
        pl.semaphore_wait(turn, 1)
        a_far[1].start()

    class Total:
        def __init__(self, call, sums, first, rows):
            self.call, self.sums, self.first, self.quarter = call, sums, first, rows // n_y

        def rows(self, y_, count=1):
            return pl.ds(pl.multiple_of(self.first + y_ * self.quarter, 8), count * self.quarter)

        def block(self, ref, slot):
            return ref.at[self.call, slot, pl.ds(0, self.sums), :, pl.ds(0, self.quarter)]

        def source(self, y_, count=1):
            return partial.at[pl.ds(0, self.sums), :, self.rows(y_, count)]

        def target(self, y_, count=1):
            return result.at[self.call, pl.ds(0, self.sums), :, self.rows(y_, count)]

        def wait(self, ref, sem, arrival):
            copy = pltpu.make_async_remote_copy(ref, ref, sem, sem, device_id=at(sibling), device_id_type=MESH)
            (copy.wait_recv if arrival else copy.wait_send)()

        def seven(self):
            return self.block(parts, pl.ds(1, 2 * n_y - 1))

        def gather(self, step):
            to = lax.rem(y + step, n_y)
            return pltpu.make_async_remote_copy(
                src_ref=self.source(to),
                dst_ref=self.block(parts, jnp.where(reducer, 0, n_y) + step),
                send_sem=in_send.at[self.call % 3],
                recv_sem=in_recv.at[self.call % 3],
                device_id=at(chip + zl, to),
                device_id_type=MESH,
            )

        def swap(self):
            return pltpu.make_async_remote_copy(
                src_ref=self.block(half_sum, slice(None)),
                dst_ref=self.block(half_in, slice(None)),
                send_sem=mid_send.at[self.call % 3],
                recv_sem=mid_recv.at[self.call % 3],
                device_id=at(sibling, zl_=1 - zl),
                device_id_type=MESH,
            )

        def spread(self, step, group):
            return pltpu.make_async_remote_copy(
                src_ref=self.block(total, group),
                dst_ref=self.target(y),
                send_sem=out_send.at[self.call % 3],
                recv_sem=out_recv.at[self.call % 3],
                device_id=at(sibling if group else gz, lax.rem(y + step, n_y)),
                device_id_type=MESH,
            )

        def send(self):
            for step in SPREAD:
                self.gather(step).start()

            @pl.when(jnp.logical_not(reducer))
            def _():
                self.gather(0).start()

        def reduce(self):
            @pl.when(reducer)
            def _():
                own = self.source(y)[...]
                self.wait(self.seven(), in_recv.at[self.call % 3], True)
                for group in range(2):
                    block = self.block(parts, n_y)[...] if group else own
                    for step in range(1, n_y):
                        block = block + self.block(parts, group * n_y + step)[...]
                    self.block(half_sum, group)[...] = block
                self.swap().start()

        def finish(self):
            @pl.when(reducer)
            def _():
                self.swap().wait_recv()
                for group in range(2):
                    block = self.block(half_sum, group)[...] + self.block(half_in, 1 - group)[...]
                    self.block(total, group)[...] = block
                    if group == 0:
                        self.target(y)[...] = block
                for step in SPREAD:
                    for group in range(2):
                        self.spread(step, group).start()
                self.spread(0, 1).start()

        def arrive(self):
            for others, count in ((reducer, n_y - 1), (jnp.logical_not(reducer), n_y)):

                @pl.when(others)
                def _():
                    self.wait(self.target(0, count), out_recv.at[self.call % 3], True)

        def drain(self):
            for others, count in ((reducer, n_y - 1), (jnp.logical_not(reducer), n_y)):

                @pl.when(others)
                def _():
                    self.wait(self.source(0, count), in_send.at[self.call % 3], False)

            @pl.when(reducer)
            def _():
                self.swap().wait_send()
                self.wait(self.seven(), out_send.at[self.call % 3], False)

    squares_first = Total(0, 1, 0, nx)
    second = [Total(1 + h, 2, h * half_rows, half_rows) for h in range(HALVES)]
    coupled_first = [Total(1 + HALVES + h, 1, h * half_rows, half_rows) for h in range(HALVES)]

    loads[0].wait()
    for z in range(planes):

        def add_square(p, acc):
            value = u[p, z]
            return acc + value * value

        partial[0, z] = lax.fori_loop(0, order, add_square, jnp.zeros((nx, ny), jnp.float32))
    squares_first.send()
    a_near.start()

    loads[2].wait()
    loads[3].wait()

    def own_middle(i, _):
        p, z = i // planes, lax.rem(i, planes)
        value = u[p, z]
        m, k = rate[p], stiff[p]
        slope = (1.0 + m) - (m * (1.0 - 2.0 * COUPLE)) * (value * value)
        mid[p, z] = value * slope + (m * k) * flat_laplacian(value, u[p, 1 - z])
        return 0

    lax.fori_loop(0, order * planes, own_middle, 0)
    loads[1].wait()

    def own_adjoint(i, _):
        p, z = i // planes, lax.rem(i, planes)
        value = a[p, z]
        m, k = rate[p], stiff[p]
        adj[p, z] = (1.0 + m) * value + (m * k) * flat_laplacian(value, a[p, 1 - z])
        return 0

    lax.fori_loop(0, order, own_adjoint, 0)
    squares_first.reduce()
    lax.fori_loop(order, order * planes, own_adjoint, 0)
    squares_first.finish()
    squares_first.arrive()
    squares_first.drain()

    def middle_half(h):
        rows = half(h)
        u_far[h].wait_recv()
        for z in range(planes):
            weight = (2.0 * COUPLE) * result[0, 0, z, rows]

            def middle(p, carry):
                squares, coupled = carry
                m, k = rate[p], stiff[p]
                value = mid[p, z, rows] - m * (u[p, z, rows] * weight)
                value = value + (m * k) * u_halo[p, z, rows]
                mid[p, z, rows] = value
                return squares + value * value, coupled + value * (m * a[p, z, rows])

            zero = jnp.zeros((half_rows, ny), jnp.float32)
            squares, coupled = lax.fori_loop(0, order, middle, (zero, zero))
            partial[0, z, rows] = squares
            partial[1, z, rows] = coupled
        second[h].send()

    def adjoint_half(h):
        rows = half(h)
        a_far[h].wait_recv()
        for z in range(planes):
            weight = (2.0 * COUPLE) * result[1 + h, 0, z, rows]
            pull = (4.0 * COUPLE) * result[1 + h, 1, z, rows]

            def adjoint(p, acc):
                m, k = rate[p], stiff[p]
                field = mid[p, z, rows]
                value = adj[p, z, rows] - (m * a[p, z, rows]) * (CUBE * (field * field) + weight)
                value = value - field * pull + (m * k) * a_halo[p, z, rows]
                adj[p, z, rows] = value
                scaled = m * value
                w[p, z, rows] = k * scaled
                return acc + u[p, z, rows] * scaled

            partial[0, z, rows] = lax.fori_loop(
                0, order, adjoint, jnp.zeros((half_rows, ny), jnp.float32)
            )
        if h == 0:
            w_far[0].start()
        else:
            pl.when(jnp.logical_not(reducer))(w_far[1].start)
        w_near[h].start()
        coupled_first[h].send()

    u_near.wait_recv()
    middle_half(0)
    second[0].reduce()
    yield_link()
    middle_half(1)
    second[0].finish()
    second[1].reduce()
    second[0].arrive()
    second[0].drain()
    second[1].finish()
    a_near.wait_recv()
    adjoint_half(0)
    second[1].arrive()
    second[1].drain()
    adjoint_half(1)
    coupled_first[0].reduce()

    def own_result(i, _):
        p, z = i // planes, lax.rem(i, planes)
        value, full = u[p, z], adj[p, z]
        slope = CUBE * (value * value) + (2.0 * COUPLE) * result[0, 0, z]
        local = full + (rate[p] * full) * (1.0 - slope)
        adj[p, z] = local + flat_laplacian(w[p, z], w[p, 1 - z])
        return 0

    lax.fori_loop(0, order * planes, own_result, 0)
    coupled_first[1].reduce()

    @pl.when(reducer)
    def _():
        pl.semaphore_wait(turn, 1)
        w_far[1].start()

    @pl.when(jnp.logical_not(reducer))
    def _():
        w_far[0].wait_send()
        pl.semaphore_signal(turn, inc=1, device_id=at(zl_=1 - zl), device_id_type=MESH)

    coupled_first[0].finish()
    coupled_first[1].finish()
    for h in range(HALVES):
        rows = half(h)
        coupled_first[h].arrive()
        for z in range(planes):
            pull = (4.0 * COUPLE) * result[1 + HALVES + h, 0, z, rows]

            def couple(p, _):
                adj[p, z, rows] = adj[p, z, rows] - u[p, z, rows] * pull
                return 0

            lax.fori_loop(0, order, couple, 0)
    store = pltpu.make_async_copy(adj, part, store_sem)
    store.start()
    for h in range(HALVES):
        coupled_first[h].drain()
    for copy in a_far + [u_near, a_near]:
        copy.wait_send()
    for copy in w_near + [w_far[1]]:
        copy.wait()
    w_far[0].wait_recv()

    @pl.when(reducer)
    def _():
        w_far[0].wait_send()
    store.wait()


def add_halo(part, w_halo, out, whole, sem):
    order = whole.shape[0]

    def one(p, _):
        whole[p] = part[p] + w_halo[p]
        pltpu.make_async_copy(whole.at[p], out.at[p], sem).start()
        return 0

    lax.fori_loop(0, order, one, 0)
    pltpu.make_async_copy(whole, out, sem).wait()


def on_device(n_gz, n_ord, initial, cotangent, mobility, stiffness):
    shape = initial.shape
    order, planes, nx, ny = shape
    n_y = n_ord // 2
    calls = 1 + 2 * HALVES
    f32 = jnp.float32
    field = jax.ShapeDtypeStruct(shape, f32)
    quarter = nx // n_y
    part, w_halo = pl.pallas_call(
        functools.partial(kernel, n_gz, n_y),
        out_shape=(field, field),
        in_specs=[pl.BlockSpec(memory_space=pltpu.HBM)] * 4,
        out_specs=[pl.BlockSpec(memory_space=pl.ANY)] * 2,
        scratch_shapes=[pltpu.SMEM((order,), f32)] * 2
        + [pltpu.VMEM(shape, f32)] * 7
        + [
            pltpu.VMEM((2, planes, nx, ny), f32),
            pltpu.VMEM((calls, 2 * n_y, 2, planes, quarter, ny), f32),
            pltpu.VMEM((calls, 2, 2, planes, quarter, ny), f32),
            pltpu.VMEM((calls, 2, 2, planes, quarter, ny), f32),
            pltpu.VMEM((calls, 2, 2, planes, quarter, ny), f32),
            pltpu.VMEM((calls, 2, planes, nx, ny), f32),
            pltpu.SemaphoreType.DMA((4,)),
            pltpu.SemaphoreType.DMA((3 * HALVES,)),
            pltpu.SemaphoreType.DMA((3 * HALVES,)),
            pltpu.SemaphoreType.DMA((2 + HALVES,)),
            pltpu.SemaphoreType.DMA((2 + HALVES,)),
        ]
        + [pltpu.SemaphoreType.DMA((3,))] * 6
        + [
            pltpu.SemaphoreType.DMA,
            pltpu.SemaphoreType.REGULAR,
        ],
        compiler_params=pltpu.CompilerParams(
            collective_id=0, has_side_effects=True, vmem_limit_bytes=32 << 20
        ),
        name="adjoint_steps",
    )(*(pltpu.with_memory_space_constraint(x, pltpu.HBM) for x in (initial, cotangent, mobility, stiffness)))
    return pl.pallas_call(
        add_halo,
        out_shape=field,
        in_specs=[pl.BlockSpec(memory_space=pltpu.VMEM)] * 2,
        out_specs=pl.BlockSpec(memory_space=pltpu.HBM),
        scratch_shapes=[pltpu.VMEM(shape, f32), pltpu.SemaphoreType.DMA],
        compiler_params=pltpu.CompilerParams(vmem_limit_bytes=16 << 20),
        name="add_halo",
    )(part, w_halo)


def solution(mesh):
    return jax.shard_map(
        functools.partial(on_device, mesh.shape["gz"], mesh.shape["ord"]),
        mesh=mesh,
        in_specs=(P("ord", "gz", None, None), P("ord", "gz", None, None), P("ord"), P("ord")),
        out_specs=P("ord", "gz", None, None),
        check_vma=False,
    )
```

```python
import functools

import jax
import jax.numpy as jnp
from jax import lax
from jax.experimental import pallas as pl
from jax.experimental.pallas import tpu as pltpu
from jax.sharding import PartitionSpec as P

P_SIZE = 96
COUPLE = 2.0 / P_SIZE
CUBE = 3.0 - 6.0 * COUPLE
MESH = pl.DeviceIdType.MESH
HALVES = 2
SPREAD = (2, 1, 3)


def flat_laplacian(plane, other):
    rows, cols = plane.shape
    side = pltpu.roll(plane, 1, 0) + pltpu.roll(plane, rows - 1, 0)
    side = side + (pltpu.roll(plane, 1, 1) + pltpu.roll(plane, cols - 1, 1))
    return side + (other - 6.0 * plane)


def kernel(
    n_gz, n_y,
    u_hbm, a_hbm, rate_hbm, stiff_hbm,
    part, w_halo,
    rate, stiff, u, a, mid, adj, w, u_halo, a_halo, partial, parts, half_sum, half_in, total, result,
    load_sem, far_send, far_recv, near_send, near_recv,
    in_send, in_recv, mid_send, mid_recv, out_send, out_recv, store_sem, turn,
):
    order, planes, nx, ny = u.shape
    gz, ord_ = lax.axis_index("gz"), lax.axis_index("ord")
    core, y, zl = lax.rem(gz, 2), ord_ // 2, lax.rem(ord_, 2)
    sibling = gz + 1 - 2 * core
    chip = gz - core
    far = lax.rem(jnp.where(core == 1, gz + 1, gz + n_gz - 1), n_gz)
    far_plane, near_plane = core, 1 - core
    reducer = core == zl
    half_rows = nx // HALVES

    def at(gz_=None, y_=None, zl_=None):
        y_ = y if y_ is None else y_
        zl_ = zl if zl_ is None else zl_
        return {"gz": gz if gz_ is None else gz_, "ord": 2 * y_ + zl_}

    loads = [
        pltpu.make_async_copy(u_hbm, u, load_sem.at[0]),
        pltpu.make_async_copy(a_hbm, a, load_sem.at[1]),
        pltpu.make_async_copy(rate_hbm, rate, load_sem.at[2]),
        pltpu.make_async_copy(stiff_hbm, stiff, load_sem.at[3]),
    ]
    for copy in loads:
        copy.start()

    barrier = pltpu.get_barrier_semaphore()
    peers = [at(far), at(sibling, zl_=1 - zl), at(sibling), at(zl_=1 - zl)]
    for step in range(1, n_y):
        for c in range(2):
            peers.append(at(chip + c, lax.rem(y + step, n_y)))
    for peer in peers:
        pl.semaphore_signal(barrier, inc=1, device_id=peer, device_id_type=MESH)
    pl.semaphore_wait(barrier, len(peers))

    def halo(index, src, dst, far_side, rows):
        mine = far_plane if far_side else near_plane
        theirs = 1 - mine
        return pltpu.make_async_remote_copy(
            src_ref=src.at[:, mine, rows],
            dst_ref=dst.at[:, theirs, rows],
            send_sem=(far_send if far_side else near_send).at[index],
            recv_sem=(far_recv if far_side else near_recv).at[index],
            device_id=at(far if far_side else sibling),
            device_id_type=MESH,
        )

    def half(h):
        return pl.ds(h * half_rows, half_rows)

    u_far = [halo(h, u_hbm, u_halo, True, half(h)) for h in range(HALVES)]
    a_far = [halo(HALVES + h, a_hbm, a_halo, True, half(h)) for h in range(HALVES)]
    w_far = [halo(2 * HALVES + h, w, w_halo, True, half(h)) for h in range(HALVES)]
    u_near = halo(0, u_hbm, u_halo, False, pl.ds(0, nx))
    a_near = halo(1, a_hbm, a_halo, False, pl.ds(0, nx))
    w_near = [halo(2 + h, w, w_halo, False, half(h)) for h in range(HALVES)]
    for copy in u_far + [u_near]:
        copy.start()

    a_far[0].start()

    def yield_link():
        for copy in u_far:
            copy.wait_send()
        pl.semaphore_signal(turn, inc=1, device_id=at(zl_=1 - zl), device_id_type=MESH)
        pl.semaphore_wait(turn, 1)
        a_far[1].start()

    class Total:
        def __init__(self, call, sums, first, rows):
            self.call, self.sums, self.first, self.quarter = call, sums, first, rows // n_y

        def rows(self, y_, count=1):
            return pl.ds(pl.multiple_of(self.first + y_ * self.quarter, 8), count * self.quarter)

        def block(self, ref, slot):
            return ref.at[self.call, slot, pl.ds(0, self.sums), :, pl.ds(0, self.quarter)]

        def source(self, y_, count=1):
            return partial.at[pl.ds(0, self.sums), :, self.rows(y_, count)]

        def target(self, y_, count=1):
            return result.at[self.call, pl.ds(0, self.sums), :, self.rows(y_, count)]

        def wait(self, ref, sem, arrival):
            copy = pltpu.make_async_remote_copy(ref, ref, sem, sem, device_id=at(sibling), device_id_type=MESH)
            (copy.wait_recv if arrival else copy.wait_send)()

        def seven(self):
            return self.block(parts, pl.ds(1, 2 * n_y - 1))

        def gather(self, step):
            to = lax.rem(y + step, n_y)
            return pltpu.make_async_remote_copy(
                src_ref=self.source(to),
                dst_ref=self.block(parts, jnp.where(reducer, 0, n_y) + step),
                send_sem=in_send.at[self.call % 3],
                recv_sem=in_recv.at[self.call % 3],
                device_id=at(chip + zl, to),
                device_id_type=MESH,
            )

        def swap(self):
            return pltpu.make_async_remote_copy(
                src_ref=self.block(half_sum, slice(None)),
                dst_ref=self.block(half_in, slice(None)),
                send_sem=mid_send.at[self.call % 3],
                recv_sem=mid_recv.at[self.call % 3],
                device_id=at(sibling, zl_=1 - zl),
                device_id_type=MESH,
            )

        def spread(self, step, group):
            return pltpu.make_async_remote_copy(
                src_ref=self.block(total, group),
                dst_ref=self.target(y),
                send_sem=out_send.at[self.call % 3],
                recv_sem=out_recv.at[self.call % 3],
                device_id=at(sibling if group else gz, lax.rem(y + step, n_y)),
                device_id_type=MESH,
            )

        def send(self):
            for step in SPREAD:
                self.gather(step).start()

            @pl.when(jnp.logical_not(reducer))
            def _():
                self.gather(0).start()

        def reduce(self):
            @pl.when(reducer)
            def _():
                own = self.source(y)[...]
                self.wait(self.seven(), in_recv.at[self.call % 3], True)
                for group in range(2):
                    block = self.block(parts, n_y)[...] if group else own
                    for step in range(1, n_y):
                        block = block + self.block(parts, group * n_y + step)[...]
                    self.block(half_sum, group)[...] = block
                self.swap().start()

        def finish(self):
            @pl.when(reducer)
            def _():
                self.swap().wait_recv()
                for group in range(2):
                    block = self.block(half_sum, group)[...] + self.block(half_in, 1 - group)[...]
                    self.block(total, group)[...] = block
                    if group == 0:
                        self.target(y)[...] = block
                for step in SPREAD:
                    for group in range(2):
                        self.spread(step, group).start()
                self.spread(0, 1).start()

        def arrive(self):
            for others, count in ((reducer, n_y - 1), (jnp.logical_not(reducer), n_y)):

                @pl.when(others)
                def _():
                    self.wait(self.target(0, count), out_recv.at[self.call % 3], True)

        def drain(self):
            for others, count in ((reducer, n_y - 1), (jnp.logical_not(reducer), n_y)):

                @pl.when(others)
                def _():
                    self.wait(self.source(0, count), in_send.at[self.call % 3], False)

            @pl.when(reducer)
            def _():
                self.swap().wait_send()
                self.wait(self.seven(), out_send.at[self.call % 3], False)

    squares_first = Total(0, 1, 0, nx)
    second = [Total(1 + h, 2, h * half_rows, half_rows) for h in range(HALVES)]
    coupled_first = [Total(1 + HALVES + h, 1, h * half_rows, half_rows) for h in range(HALVES)]

    loads[0].wait()
    for z in range(planes):

        def add_square(p, acc):
            value = u[p, z]
            return acc + value * value

        partial[0, z] = lax.fori_loop(0, order, add_square, jnp.zeros((nx, ny), jnp.float32))
    squares_first.send()
    a_near.start()

    loads[2].wait()
    loads[3].wait()

    def own_middle(i, _):
        p, z = i // planes, lax.rem(i, planes)
        value = u[p, z]
        m, k = rate[p], stiff[p]
        slope = (1.0 + m) - (m * (1.0 - 2.0 * COUPLE)) * (value * value)
        mid[p, z] = value * slope + (m * k) * flat_laplacian(value, u[p, 1 - z])
        return 0

    lax.fori_loop(0, order * planes, own_middle, 0)
    loads[1].wait()

    def own_adjoint(i, _):
        p, z = i // planes, lax.rem(i, planes)
        value = a[p, z]
        m, k = rate[p], stiff[p]
        adj[p, z] = (1.0 + m) * value + (m * k) * flat_laplacian(value, a[p, 1 - z])
        return 0

    lax.fori_loop(0, order, own_adjoint, 0)
    squares_first.reduce()
    lax.fori_loop(order, order * planes, own_adjoint, 0)
    squares_first.finish()
    squares_first.arrive()
    squares_first.drain()

    def middle_half(h):
        rows = half(h)
        u_far[h].wait_recv()
        for z in range(planes):
            weight = (2.0 * COUPLE) * result[0, 0, z, rows]

            def middle(p, carry):
                squares, coupled = carry
                m, k = rate[p], stiff[p]
                value = mid[p, z, rows] - m * (u[p, z, rows] * weight)
                value = value + (m * k) * u_halo[p, z, rows]
                mid[p, z, rows] = value
                return squares + value * value, coupled + value * (m * a[p, z, rows])

            zero = jnp.zeros((half_rows, ny), jnp.float32)
            squares, coupled = lax.fori_loop(0, order, middle, (zero, zero))
            partial[0, z, rows] = squares
            partial[1, z, rows] = coupled
        second[h].send()

    def adjoint_half(h):
        rows = half(h)
        a_far[h].wait_recv()
        for z in range(planes):
            weight = (2.0 * COUPLE) * result[1 + h, 0, z, rows]
            pull = (4.0 * COUPLE) * result[1 + h, 1, z, rows]

            def adjoint(p, acc):
                m, k = rate[p], stiff[p]
                field = mid[p, z, rows]
                value = adj[p, z, rows] - (m * a[p, z, rows]) * (CUBE * (field * field) + weight)
                value = value - field * pull + (m * k) * a_halo[p, z, rows]
                adj[p, z, rows] = value
                scaled = m * value
                w[p, z, rows] = k * scaled
                return acc + u[p, z, rows] * scaled

            partial[0, z, rows] = lax.fori_loop(
                0, order, adjoint, jnp.zeros((half_rows, ny), jnp.float32)
            )
        if h == 0:
            w_far[0].start()
        else:
            pl.when(jnp.logical_not(reducer))(w_far[1].start)
        w_near[h].start()
        coupled_first[h].send()

    u_near.wait_recv()
    middle_half(0)
    second[0].reduce()
    yield_link()
    middle_half(1)
    second[0].finish()
    second[1].reduce()
    second[0].arrive()
    second[0].drain()
    second[1].finish()
    a_near.wait_recv()
    adjoint_half(0)
    second[1].arrive()
    second[1].drain()
    adjoint_half(1)
    coupled_first[0].reduce()

    def own_result(i, _):
        p, z = i // planes, lax.rem(i, planes)
        value, full = u[p, z], adj[p, z]
        slope = CUBE * (value * value) + (2.0 * COUPLE) * result[0, 0, z]
        local = full + (rate[p] * full) * (1.0 - slope)
        adj[p, z] = local + flat_laplacian(w[p, z], w[p, 1 - z])
        return 0

    lax.fori_loop(0, order * planes, own_result, 0)
    coupled_first[1].reduce()

    @pl.when(reducer)
    def _():
        pl.semaphore_wait(turn, 1)
        w_far[1].start()

    @pl.when(jnp.logical_not(reducer))
    def _():
        w_far[0].wait_send()
        pl.semaphore_signal(turn, inc=1, device_id=at(zl_=1 - zl), device_id_type=MESH)

    coupled_first[0].finish()
    coupled_first[1].finish()
    for h in range(HALVES):
        rows = half(h)
        coupled_first[h].arrive()
        for z in range(planes):
            pull = (4.0 * COUPLE) * result[1 + HALVES + h, 0, z, rows]

            def couple(p, _):
                adj[p, z, rows] = adj[p, z, rows] - u[p, z, rows] * pull
                return 0

            lax.fori_loop(0, order, couple, 0, unroll=2)
    store = pltpu.make_async_copy(adj, part, store_sem)
    store.start()
    for h in range(HALVES):
        coupled_first[h].drain()
    for copy in a_far + [u_near, a_near]:
        copy.wait_send()
    for copy in w_near + [w_far[1]]:
        copy.wait()
    w_far[0].wait_recv()

    @pl.when(reducer)
    def _():
        w_far[0].wait_send()
    store.wait()


def add_halo(part, w_halo, out, whole, sem):
    order = whole.shape[0]

    def one(p, _):
        whole[p] = part[p] + w_halo[p]
        pltpu.make_async_copy(whole.at[p], out.at[p], sem).start()
        return 0

    lax.fori_loop(0, order, one, 0, unroll=True)
    pltpu.make_async_copy(whole, out, sem).wait()


def on_device(n_gz, n_ord, initial, cotangent, mobility, stiffness):
    shape = initial.shape
    order, planes, nx, ny = shape
    n_y = n_ord // 2
    calls = 1 + 2 * HALVES
    f32 = jnp.float32
    field = jax.ShapeDtypeStruct(shape, f32)
    quarter = nx // n_y
    part, w_halo = pl.pallas_call(
        functools.partial(kernel, n_gz, n_y),
        out_shape=(field, field),
        in_specs=[pl.BlockSpec(memory_space=pltpu.HBM)] * 4,
        out_specs=[pl.BlockSpec(memory_space=pl.ANY)] * 2,
        scratch_shapes=[pltpu.SMEM((order,), f32)] * 2
        + [pltpu.VMEM(shape, f32)] * 7
        + [
            pltpu.VMEM((2, planes, nx, ny), f32),
            pltpu.VMEM((calls, 2 * n_y, 2, planes, quarter, ny), f32),
            pltpu.VMEM((calls, 2, 2, planes, quarter, ny), f32),
            pltpu.VMEM((calls, 2, 2, planes, quarter, ny), f32),
            pltpu.VMEM((calls, 2, 2, planes, quarter, ny), f32),
            pltpu.VMEM((calls, 2, planes, nx, ny), f32),
            pltpu.SemaphoreType.DMA((4,)),
            pltpu.SemaphoreType.DMA((3 * HALVES,)),
            pltpu.SemaphoreType.DMA((3 * HALVES,)),
            pltpu.SemaphoreType.DMA((2 + HALVES,)),
            pltpu.SemaphoreType.DMA((2 + HALVES,)),
        ]
        + [pltpu.SemaphoreType.DMA((3,))] * 6
        + [
            pltpu.SemaphoreType.DMA,
            pltpu.SemaphoreType.REGULAR,
        ],
        compiler_params=pltpu.CompilerParams(
            collective_id=0, has_side_effects=True, vmem_limit_bytes=32 << 20
        ),
        name="adjoint_steps",
    )(*(pltpu.with_memory_space_constraint(x, pltpu.HBM) for x in (initial, cotangent, mobility, stiffness)))
    return pl.pallas_call(
        add_halo,
        out_shape=field,
        in_specs=[pl.BlockSpec(memory_space=pltpu.VMEM)] * 2,
        out_specs=pl.BlockSpec(memory_space=pltpu.HBM),
        scratch_shapes=[pltpu.VMEM(shape, f32), pltpu.SemaphoreType.DMA],
        compiler_params=pltpu.CompilerParams(vmem_limit_bytes=16 << 20),
        name="add_halo",
    )(part, w_halo)


def solution(mesh):
    return jax.shard_map(
        functools.partial(on_device, mesh.shape["gz"], mesh.shape["ord"]),
        mesh=mesh,
        in_specs=(P("ord", "gz", None, None), P("ord", "gz", None, None), P("ord"), P("ord")),
        out_specs=P("ord", "gz", None, None),
        check_vma=False,
    )
```
